768 devices in a mesh: outer: 12 (over z), inner: 2 (over core), heads: 32 (over y, x).
Axes of the slice: x: 4, y: 8, z: 12, core: 2. Of those that a mesh axis runs over, the one named last changes fastest.
Arguments:
- lin_query: bfloat16 [3072, 8192], P(('outer', 'inner'), 'heads'), may hold values from -6 to 6
- lin_key: bfloat16 [3072, 8192], P(('outer', 'inner'), 'heads'), may hold values from -6 to 6
- lin_value: bfloat16 [3072, 8192], P(('outer', 'inner'), 'heads'), may hold values from -18 to 18
- gate_input: bfloat16 [3072, 8192], P(('outer', 'inner'), 'heads'), may hold values from -6 to 6
- norm_gain: bfloat16 [8192], P('heads'), may hold values from 0.099609375 to 1.8984375
- segment_ids: int32 [3072], P(('outer', 'inner')), may hold values from 0 to 15, never falling along the last dimension, each value on 1 to 384 neighbouring positions
- soft_query: bfloat16 [3072, 8192], P(('outer', 'inner'), 'heads'), may hold values from -10 to 10
- soft_key: bfloat16 [3072, 8192], P(('outer', 'inner'), 'heads'), may hold values from -4 to 4
Outputs:
- linear_out: bfloat16 [3072, 8192], P(('outer', 'inner'), 'heads')
- attended: bfloat16 [3072, 8192], P(('outer', 'inner'), 'heads')
The draws below stay inside these ranges and needn't reach their ends.
Inputs may be any that keep to these rules, and one draw needn't show every extreme that they name: `segment_ids`: numbers never fall along the sequence, every number from 0 to 15 is used, and a document has at most 384 tokens.
All inputs are finite; a program needn't handle non-finite values.
Results may differ from the reference program's by a relative error of at most 0.0062.
Values may be sent and summed in bfloat16 or wider, within the bound.
A program may use at most 32 MiB of HBM per device.

```python
import math
import jax
import jax.numpy as jnp
import numpy as np
from jax import lax

H = 64
DH = 128
TOK_DEV = 128
SPAN = 3
SEQ = 3072
MOSTDOC = 384
DOCS = 16


def draw_lin_value(key, part):
    ramp = jnp.arange(H, dtype=jnp.float32) / (H - 1)
    base = jnp.clip(jax.random.normal(key, (SEQ, H, DH), jnp.float32), -4.0, 4.0)
    scales = 3.0 ** ramp
    return (base * scales[None, :, None]).reshape(SEQ, H * DH).astype(jnp.bfloat16)


def draw_soft_key(key, part):
    base = jnp.clip(jax.random.normal(jax.random.fold_in(key, 1), (SEQ, H, DH), jnp.float32), -4.0, 4.0)
    return base.reshape(SEQ, H * DH).astype(jnp.bfloat16)


def draw_soft_query(key, part):
    base = jnp.clip(jax.random.normal(jax.random.fold_in(key, 2), (SEQ, H, DH), jnp.float32), -4.0, 4.0)
    return base.reshape(SEQ, H * DH).astype(jnp.bfloat16)


def block_scale(own_key, shape, pieces, low, high):
    gain, own = 1.0, jax.random.fold_in(own_key, 6)
    for axis_at, parts in pieces:
        draws = jnp.exp(jax.random.uniform(jax.random.fold_in(own, axis_at), (parts,), jnp.float32, low / len(pieces), high / len(pieces)))
        gain = gain * jnp.repeat(draws, shape[axis_at] // parts).reshape([-1 if axis == axis_at else 1 for axis in range(len(shape))])
    return gain


def split_up(amount, total, reach, slope):
    portions = [(1 << 20) // math.isqrt(standing ** slope) + 1 for standing in range(2, amount + 1)]
    spare, holding = total - reach - (amount - 1), [1] * (amount - 1)
    while spare > 0:
        free = [i for i in range(amount - 1) if holding[i] < reach]
        mass, left = sum([portions[i] for i in free]), spare
        for i in free:
            addition = min(reach - holding[i], max(1, left * portions[i] // mass), spare)
            holding[i] = holding[i] + addition
            spare = spare - addition
    return np.array([reach] + holding)


def uneven(rng, count, total, most, lean):
    if count == 2:
        one = jax.random.randint(rng, (), max(1, total - most), min(most, total - 1) + 1)
        return jnp.stack([one, total - one])
    tallies = jnp.asarray(split_up(count, total, most, lean), jnp.int32)
    pairs = (count - 1) // 2
    donor, sink = tallies[1:1 + 2 * pairs:2], tallies[2:2 + 2 * pairs:2]
    room = jnp.minimum(donor - 1, most - sink)
    passed = jax.random.randint(jax.random.fold_in(rng, 1), (pairs,), 0, 1 << 20) % (room + 1)
    tallies = tallies.at[1:1 + 2 * pairs:2].set(donor - passed).at[2:2 + 2 * pairs:2].set(sink + passed)
    return tallies[jax.random.permutation(jax.random.fold_in(rng, 2), count)]


def noise(rng, extent, width, reach, cuts=(), kind=jnp.bfloat16):
    result = jax.random.normal(rng, extent, jnp.float32) * width
    if len(cuts) > 0:
        result = block_scale(rng, extent, cuts, -0.22, 0.18) * result
    return jnp.clip(result, min=-reach, max=reach).astype(kind)


def setup_inputs(seed: int = 0) -> dict:
    key_list = jax.random.split(jax.random.key(seed), 9)
    lin_query = noise(key_list[0], (SEQ, H * DH), 1.0, 6.0, ((0, 24), (1, 32)))
    lin_key = noise(key_list[1], (SEQ, H * DH), 1.0, 6.0, ((0, 24), (1, 32)))
    lin_value = draw_lin_value(jax.random.fold_in(key_list[8], 71), 0)
    gate_input = noise(key_list[3], (SEQ, H * DH), 1.0, 6.0, ((0, 24), (1, 32)))
    norm_gain = jnp.clip(1.0 + 0.18 * jax.random.normal(key_list[4], (H * DH,), jnp.float32), 0.099609375, 1.8984375).astype(jnp.bfloat16)
    segment_ids = jnp.searchsorted(jnp.cumsum(uneven(key_list[5], DOCS, SEQ, MOSTDOC, 2)), jnp.arange(SEQ), side="right").astype(jnp.int32)
    soft_query = draw_soft_query(jax.random.fold_in(key_list[8], 71), 0)
    soft_key = draw_soft_key(jax.random.fold_in(key_list[8], 71), 0)
    return {"lin_query": lin_query, "lin_key": lin_key, "lin_value": lin_value, "gate_input": gate_input, "norm_gain": norm_gain, "segment_ids": segment_ids, "soft_query": soft_query, "soft_key": soft_key}


def reference(lin_query, lin_key, lin_value, gate_input, norm_gain, segment_ids, soft_query, soft_key):
    block_count = SEQ // TOK_DEV
    head_shape = (block_count, TOK_DEV, H, DH)
    queries = lin_query.reshape(head_shape)
    key_blocks = lin_key.reshape(head_shape)
    value_blocks = lin_value.reshape(head_shape)
    gate_blocks = gate_input.reshape(head_shape)
    documents = segment_ids.astype(jnp.int32).reshape(block_count, TOK_DEV)
    gain_cols = norm_gain.astype(jnp.float32).reshape(1, H, DH)
    token_index = jnp.arange(TOK_DEV, dtype=jnp.int32)
    causal = token_index[:, None] >= token_index[None, :]

    def linear_block(carried_in, block_item):
        carried_state, carried_doc = carried_in
        q_rows, k_rows, v_rows, g_rows, doc_rows = block_item
        q_float = q_rows.astype(jnp.float32)
        k_float = k_rows.astype(jnp.float32)
        v_float = v_rows.astype(jnp.float32)
        raw_scores = jnp.einsum('thd,shd->hts', q_float, k_float)
        visible = causal & (doc_rows[:, None] == doc_rows[None, :])
        intra_weights = lax.optimization_barrier(jnp.where(visible[None], raw_scores, 0.0).astype(jnp.bfloat16)).astype(jnp.float32)
        intra_part = jnp.einsum('hts,shd->thd', intra_weights, v_float)
        carried_part = jnp.einsum('thd,hde->the', q_float, carried_state, precision=lax.Precision.HIGHEST)
        mixed = intra_part + jnp.where((doc_rows == carried_doc)[:, None, None], carried_part, 0.0)
        mean_square = lax.optimization_barrier(jnp.mean(mixed * mixed, axis=(1, 2)))
        linear_rows = (mixed * lax.rsqrt(mean_square + 1e-05)[:, None, None] * gain_cols * jax.nn.sigmoid(g_rows.astype(jnp.float32))).astype(jnp.bfloat16)
        final_doc = doc_rows[-1]
        kept = jnp.where((doc_rows == final_doc)[:, None, None], k_float, 0.0)
        block_state = jnp.einsum('thd,the->hde', kept, v_float)
        next_state = block_state + jnp.where(carried_doc == final_doc, carried_state, 0.0)
        return ((next_state, final_doc), linear_rows)
    start_state = (jnp.zeros((H, DH, DH), jnp.float32), jnp.array(-1, jnp.int32))
    _, linear_blocks = lax.scan(linear_block, start_state, (queries, key_blocks, value_blocks, gate_blocks, documents))
    linear_out = linear_blocks.reshape(SEQ, H * DH)
    margin = SPAN * TOK_DEV
    padded_keys = jnp.concatenate([jnp.zeros((margin, H, DH), soft_key.dtype), soft_key.reshape(SEQ, H, DH)], axis=0)
    padded_values = jnp.concatenate([jnp.zeros((margin, H, DH), linear_out.dtype), linear_out.reshape(SEQ, H, DH)], axis=0)
    padded_docs = jnp.concatenate([jnp.full((margin,), -1, jnp.int32), segment_ids.astype(jnp.int32)])
    key_positions = jnp.arange(SEQ + margin, dtype=jnp.int32) - margin
    soft_rows = soft_query.reshape(SEQ, H, DH)
    all_docs = segment_ids.astype(jnp.int32)

    def attend(block):
        first = (block * TOK_DEV).astype(jnp.int32)
        key_rows = lax.dynamic_slice_in_dim(padded_keys, first, margin + TOK_DEV, 0)
        value_rows = lax.dynamic_slice_in_dim(padded_values, first, margin + TOK_DEV, 0)
        key_docs = lax.dynamic_slice_in_dim(padded_docs, first, margin + TOK_DEV, 0)
        key_pos = lax.dynamic_slice_in_dim(key_positions, first, margin + TOK_DEV, 0)
        query_rows = lax.dynamic_slice_in_dim(soft_rows, first, TOK_DEV, 0)
        query_docs = lax.dynamic_slice_in_dim(all_docs, first, TOK_DEV, 0)
        query_positions = first + token_index
        scores = jnp.einsum('thd,shd->hts', query_rows.astype(jnp.float32), key_rows.astype(jnp.float32)) * (1.0 / math.sqrt(DH))
        visible = (query_docs[:, None] == key_docs[None, :]) & (key_pos[None, :] <= query_positions[:, None])
        masked = jnp.where(visible[None], scores, -jnp.inf)
        row_top = lax.optimization_barrier(jnp.max(masked, axis=2, keepdims=True))
        exponent = jnp.where(visible[None], jnp.exp(masked - row_top), 0.0)
        soft_weights = lax.optimization_barrier((exponent / lax.optimization_barrier(jnp.sum(exponent, axis=2, keepdims=True))).astype(jnp.bfloat16)).astype(jnp.float32)
        return jnp.einsum('hts,shd->thd', soft_weights, value_rows.astype(jnp.float32)).astype(jnp.bfloat16)
    attended = lax.map(attend, jnp.arange(block_count, dtype=jnp.int32)).reshape(SEQ, H * DH)
    return (linear_out, attended)
```

```python
import functools
import math

import jax
import jax.numpy as jnp
from jax import lax
from jax.experimental import pallas as pl
from jax.experimental.pallas import tpu as pltpu
from jax.sharding import PartitionSpec as P

DH = 128
X_CHIPS = 4
REACH = 3
MESH = pl.DeviceIdType.MESH
F32 = jnp.float32
BF16 = jnp.bfloat16


def matmul(a, b):
    return jnp.dot(a, b, preferred_element_type=F32)


def matmul_nt(a, b):
    return lax.dot_general(a, b, (((1,), (1,)), ((), ())), preferred_element_type=F32)


def matmul_tn(a, b):
    return lax.dot_general(a, b, (((0,), (0,)), ((), ())), preferred_element_type=F32)


def column(row):
    n = row.shape[1]
    return jnp.transpose(jnp.broadcast_to(row, (n, n)))


def kernel(
    groups, x_chips, y_chips, total_columns,
    q_in, k_in, v_in, g_in, gain_in, seg_in, sq_in, sk_in,
    lin_out, att_out,
    q, k, v, g, gain, seg, sq, sk,
    docs, state, states, keys, mid, mids, own_row, rows_y, rows_x,
    gates, mixed, weights,
    load_sem, doc_send, doc_recv, state_send, state_recv, key_send, key_recv, mid_send, mid_recv,
    y_send, y_recv, x_send, x_recv,
):
    z = lax.axis_index("outer")
    c = lax.axis_index("inner")
    h = lax.axis_index("heads")
    y, x = h // x_chips, h % x_chips
    tokens = q.shape[0]
    heads = q.shape[1] // DH

    def at(dz, core, head):
        return (lax.rem(z + dz + groups, groups), core, head)

    def later(j):
        n = c + j + 2 * groups
        return lax.rem(z + n // 2, groups), n % 2

    loads = [
        pltpu.make_async_copy(a, b, load_sem.at[i])
        for i, (a, b) in enumerate(
            ((seg_in, seg), (k_in, k), (v_in, v), (q_in, q), (gain_in, gain), (g_in, g), (sk_in, sk), (sq_in, sq))
        )
    ]
    for copy in loads:
        copy.start()

    barrier = pltpu.get_barrier_semaphore()

    def greet(device):
        pl.semaphore_signal(barrier, inc=1, device_id=device, device_id_type=MESH)

    other = (z, 1 - c, h)
    greet(other)
    for d in range(1, y_chips):
        greet((z, c, lax.rem(y + d, y_chips) * x_chips + x))
    for j in range(REACH + 1):
        for d in range(x_chips):
            if j or d:
                bz, bc = later(-j)
                greet((bz, bc, y * x_chips + lax.rem(x + d, x_chips)))

    for copy in loads[:3]:
        copy.wait()
    doc_row = seg[...].astype(F32)
    doc_col = column(doc_row)
    kept = doc_col == doc_row[:, tokens - 1 :]
    for i in range(heads):
        cols = slice(i * DH, (i + 1) * DH)
        masked = jnp.where(kept, k[:, cols].astype(F32), 0.0).astype(BF16)
        state[cols, :] = matmul_tn(masked, v[:, cols]).astype(BF16)

    pl.semaphore_wait(barrier, y_chips - 1 + (REACH + 1) * x_chips)

    near = at(c, 1 - c, h)
    far = at(1 + c, 1 - c, h)
    relay_slot = 2 * c

    def send(src, dst, dst_slot, sends, sent, recvs, device):
        copy = pltpu.make_async_remote_copy(
            src_ref=src,
            dst_ref=dst.at[dst_slot],
            send_sem=sends.at[sent],
            recv_sem=recvs.at[dst_slot],
            device_id=device,
            device_id_type=MESH,
        )
        copy.start()
        return copy

    def arrived(dst, slot, recvs):
        pltpu.make_async_copy(dst.at[slot], dst.at[slot], recvs.at[slot]).wait()

    sent = []
    for j in range(REACH):
        bz, bc = later(j + 1)
        sent.append(send(seg, docs, j, doc_send, j, doc_recv, (bz, bc, h)))

    def spread(src, dst, sends, recvs):
        sent.append(send(src, dst, 0, sends, 0, recvs, near))
        sent.append(send(src, dst, 2, sends, 1, recvs, far))

    def relay(dst, sends, recvs):
        sent.append(send(dst.at[relay_slot], dst, 1, sends, 2, recvs, other))

    spread(state, states, state_send, state_recv)
    loads[6].wait()
    spread(sk, keys, key_send, key_recv)

    loads[3].wait()
    at_t = lax.broadcasted_iota(jnp.int32, (tokens, tokens), 0)
    at_s = lax.broadcasted_iota(jnp.int32, (tokens, tokens), 1)
    own_seen = (at_t >= at_s) & (doc_col == doc_row)
    for i in range(heads):
        cols = slice(i * DH, (i + 1) * DH)
        intra = jnp.where(own_seen, matmul_nt(q[:, cols], k[:, cols]), 0.0).astype(BF16)
        mixed[:, cols] = matmul(intra, v[:, cols])
    loads[4].wait()
    loads[5].wait()
    gates[...] = jax.nn.sigmoid(g[...].astype(F32)) * gain[...].astype(F32)

    for j in range(REACH):
        arrived(docs, j, doc_recv)

    arrived(states, relay_slot, state_recv)
    relay(states, state_send, state_recv)
    arrived(states, 2 - relay_slot, state_recv)
    arrived(states, 1, state_recv)
    for i in range(heads):
        cols = slice(i * DH, (i + 1) * DH)
        q_f32 = q[:, cols].astype(F32)
        carried = None
        for j in range(REACH):
            last = docs[j].astype(F32)[:, tokens - 1 :]
            part = matmul(jnp.where(doc_col == last, q_f32, 0.0).astype(BF16), states[j, cols, :])
            carried = part if carried is None else carried + part
        mixed[:, cols] += carried

    square = mixed[...] * mixed[...]
    own_row[...] = matmul_nt(jnp.ones((8, heads * DH), BF16), square.astype(BF16))[:1]

    for d in range(1, y_chips):
        copy = pltpu.make_async_remote_copy(
            src_ref=own_row,
            dst_ref=rows_y.at[y],
            send_sem=y_send,
            recv_sem=y_recv,
            device_id=(z, c, lax.rem(y + d, y_chips) * x_chips + x),
            device_id_type=MESH,
        )
        copy.start()
    rows_y[y] = own_row[...]
    mid[...] = (mixed[...] * gates[...]).astype(BF16)
    spread(mid, mids, mid_send, mid_recv)

    loads[7].wait()
    arrived(keys, relay_slot, key_recv)
    relay(keys, key_send, key_recv)
    arrived(keys, 2 - relay_slot, key_recv)
    arrived(keys, 1, key_recv)
    scale = 1.0 / math.sqrt(DH)
    for i in range(heads):
        cols = slice(i * DH, (i + 1) * DH)
        query = sq[:, cols]
        parts = [jnp.where(own_seen, matmul_nt(query, sk[:, cols]) * scale, -jnp.inf)]
        for j in range(REACH):
            seen = doc_col == docs[j].astype(F32)
            parts.append(jnp.where(seen, matmul_nt(query, keys[j, :, cols]) * scale, -jnp.inf))
        top = parts[0]
        for part in parts[1:]:
            top = jnp.maximum(top, part)
        top = jnp.max(top, axis=1, keepdims=True)
        parts = [jnp.exp(part - top) for part in parts]
        total = jnp.sum(parts[0] + parts[1] + parts[2] + parts[3], axis=1, keepdims=True)
        for j, part in enumerate(parts):
            weights[i, j] = part / total

    if y_chips > 1:
        span = pl.ds(0, y_chips - 1)
        pltpu.make_async_copy(rows_y.at[span], rows_y.at[span], y_recv).wait()
    own_row2 = rows_x.at[0, x]
    own_row2[...] = jnp.sum(rows_y[...], axis=0)
    for j in range(REACH + 1):
        for d in range(x_chips):
            if j or d:
                bz, bc = later(j)
                copy = pltpu.make_async_remote_copy(
                    src_ref=own_row2,
                    dst_ref=rows_x.at[j, x],
                    send_sem=x_send,
                    recv_sem=x_recv.at[j],
                    device_id=(bz, bc, y * x_chips + lax.rem(x + d, x_chips)),
                    device_id_type=MESH,
                )
                copy.start()

    arrived(mids, relay_slot, mid_recv)
    relay(mids, mid_send, mid_recv)

    def inverse_norm(j):
        span = pl.ds(0, x_chips if j else x_chips - 1)
        pltpu.make_async_copy(rows_x.at[j, span], rows_x.at[j, span], x_recv.at[j]).wait()
        return lax.rsqrt(jnp.sum(rows_x[j], axis=0) / total_columns + 1e-05)

    inverse = inverse_norm(0)
    inverse_col = column(inverse)
    for i in range(heads):
        cols = slice(i * DH, (i + 1) * DH)
        lin_out[:, cols] = (mixed[:, cols] * gates[:, cols] * inverse_col).astype(BF16)

    arrived(mids, 2 - relay_slot, mid_recv)
    arrived(mids, 1, mid_recv)
    inverses = [inverse] + [inverse_norm(j + 1) for j in range(REACH)]
    for i in range(heads):
        cols = slice(i * DH, (i + 1) * DH)
        result = matmul((weights[i, 0] * inverses[0]).astype(BF16), mid[:, cols])
        for j in range(REACH):
            result += matmul((weights[i, j + 1] * inverses[j + 1]).astype(BF16), mids[j, :, cols])
        att_out[:, cols] = result.astype(BF16)

    for copy in sent:
        copy.wait_send()
    if y_chips > 1:
        span = pl.ds(0, y_chips - 1)
        pltpu.make_async_copy(rows_y.at[span], rows_y.at[span], y_send).wait()
    count = (REACH + 1) * x_chips - 1
    pltpu.make_async_copy(weights.at[0, 0, pl.ds(0, count)], weights.at[0, 0, pl.ds(0, count)], x_send).wait()


def per_device(mesh, *args):
    q, k, v, g, gain, seg, sq, sk = args
    tokens, columns = q.shape
    groups = mesh.shape["outer"]
    x_chips = min(X_CHIPS, mesh.shape["heads"])
    y_chips = mesh.shape["heads"] // x_chips
    total_columns = columns * mesh.shape["heads"]
    seg = seg.reshape(1, tokens)
    gain = gain.reshape(1, columns)
    dma = pltpu.SemaphoreType.DMA
    block = (tokens, columns)
    stacked = (columns, DH)
    return pl.pallas_call(
        functools.partial(kernel, groups, x_chips, y_chips, total_columns),
        out_shape=(jax.ShapeDtypeStruct(block, BF16), jax.ShapeDtypeStruct(block, BF16)),
        in_specs=[pl.BlockSpec(memory_space=pl.ANY)] * 8,
        out_specs=(pl.BlockSpec(memory_space=pltpu.VMEM), pl.BlockSpec(memory_space=pltpu.VMEM)),
        scratch_shapes=[
            pltpu.VMEM(block, BF16), pltpu.VMEM(block, BF16), pltpu.VMEM(block, BF16), pltpu.VMEM(block, BF16),
            pltpu.VMEM((1, columns), BF16), pltpu.VMEM((1, tokens), jnp.int32),
            pltpu.VMEM(block, BF16), pltpu.VMEM(block, BF16),
            pltpu.VMEM((REACH, 1, tokens), jnp.int32),
            pltpu.VMEM(stacked, BF16), pltpu.VMEM((REACH,) + stacked, BF16),
            pltpu.VMEM((REACH,) + block, BF16),
            pltpu.VMEM(block, BF16), pltpu.VMEM((REACH,) + block, BF16),
            pltpu.VMEM((1, tokens), F32),
            pltpu.VMEM((y_chips, 1, tokens), F32),
            pltpu.VMEM((REACH + 1, x_chips, 1, tokens), F32),
            pltpu.VMEM(block, F32), pltpu.VMEM(block, F32),
            pltpu.VMEM((columns // DH, REACH + 1, tokens, tokens), F32),
            dma((8,)),
            dma((REACH,)), dma((REACH,)), dma((3,)), dma((REACH,)), dma((3,)), dma((REACH,)), dma((3,)), dma((REACH,)),
            dma, dma, dma, dma((REACH + 1,)),
        ],
        compiler_params=pltpu.CompilerParams(collective_id=0, has_side_effects=True),
    )(q, k, v, g, gain, seg, sq, sk)


def solution(mesh):
    block = P(("outer", "inner"), "heads")
    return jax.shard_map(
        functools.partial(per_device, mesh),
        mesh=mesh,
        in_specs=(block, block, block, block, P("heads"), P(("outer", "inner")), block, block),
        out_specs=(block, block),
        check_vma=False,
    )
```

```python
import functools
import math

import jax
import jax.numpy as jnp
from jax import lax
from jax.experimental import pallas as pl
from jax.experimental.pallas import tpu as pltpu
from jax.sharding import PartitionSpec as P

DH = 128
X_CHIPS = 4
REACH = 3
MESH = pl.DeviceIdType.MESH
F32 = jnp.float32
BF16 = jnp.bfloat16


def matmul(a, b):
    return jnp.dot(a, b, preferred_element_type=F32)


def matmul_nt(a, b):
    return lax.dot_general(a, b, (((1,), (1,)), ((), ())), preferred_element_type=F32)


def matmul_tn(a, b):
    return lax.dot_general(a, b, (((0,), (0,)), ((), ())), preferred_element_type=F32)


def column(row):
    n = row.shape[1]
    return jnp.transpose(jnp.broadcast_to(row, (n, n)))


def kernel(
    groups, x_chips, y_chips, total_columns,
    q_in, k_in, v_in, g_in, gain_in, seg_in, sq_in, sk_in,
    lin_out, att_out,
    q, k, v, g, gain, seg, sq, sk,
    docs, state, states, keys, mid, mids, own_row, rows_y, rows_x,
    gates, mixed, weights,
    load_sem, doc_send, doc_recv, state_send, state_recv, key_send, key_recv, mid_send, mid_recv,
    y_send, y_recv, x_send, x_recv,
):
    z = lax.axis_index("outer")
    c = lax.axis_index("inner")
    h = lax.axis_index("heads")
    y, x = h // x_chips, h % x_chips
    block = 2 * z + c
    blocks = 2 * groups
    tokens = q.shape[0]
    heads = q.shape[1] // DH
    head_cols = [slice(i * DH, (i + 1) * DH) for i in range(heads)]

    def place(n):
        return n // 2, n % 2

    def row_head(d):
        return y * x_chips + lax.rem(x + d, x_chips)

    def column_head(d):
        return lax.rem(y + d, y_chips) * x_chips + x

    loads = [
        pltpu.make_async_copy(a, b, load_sem.at[i])
        for i, (a, b) in enumerate(
            ((seg_in, seg), (k_in, k), (v_in, v), (q_in, q), (gain_in, gain), (g_in, g), (sk_in, sk), (sq_in, sq))
        )
    ]
    for copy in loads:
        copy.start()

    barrier = pltpu.get_barrier_semaphore()

    def greet(device):
        pl.semaphore_signal(barrier, inc=1, device_id=device, device_id_type=MESH)

    other = (z, 1 - c, h)
    has_relay = z >= 1
    pl.when(has_relay)(lambda: greet(other))
    for j in range(REACH + 1):

        @pl.when(block >= j)
        def _(j=j):
            for d in range(0 if j else 1, x_chips):
                greet((*place(block - j), row_head(d)))

    for d in range(1, y_chips):
        greet((z, c, column_head(d)))

    for j in range(1, REACH + 1):

        @pl.when(block < j)
        def _(j=j):
            docs[j - 1] = jnp.full((1, tokens), -1, jnp.int32)
            states[j - 1] = jnp.zeros(states.shape[1:], BF16)
            keys[j - 1] = jnp.zeros(keys.shape[1:], BF16)
            mids[j - 1] = jnp.zeros(mids.shape[1:], BF16)
            rows_x[j] = jnp.zeros(rows_x.shape[1:], F32)

    for copy in loads[:3]:
        copy.wait()
    doc_row = seg[...].astype(F32)
    doc_col = column(doc_row)
    kept = doc_col == doc_row[:, tokens - 1 :]
    for cols in head_cols:
        masked = jnp.where(kept, k[:, cols].astype(F32), 0.0).astype(BF16)
        state[cols, :] = matmul_tn(masked, v[:, cols]).astype(BF16)

    after = jnp.minimum(REACH, blocks - 1 - block)
    pl.semaphore_wait(
        barrier, y_chips - 1 + x_chips - 1 + after * x_chips + has_relay.astype(jnp.int32)
    )

    waits = []

    def remote(src, dst, send_sem, recv_sem, device):
        return pltpu.make_async_remote_copy(
            src_ref=src, dst_ref=dst, send_sem=send_sem, recv_sem=recv_sem, device_id=device, device_id_type=MESH
        )

    def send(condition, *args):
        copy = remote(*args)
        pl.when(condition)(copy.start)
        waits.append((condition, copy))

    def arrived(condition, dst, slot, recvs):
        pl.when(condition)(pltpu.make_async_copy(dst.at[slot], dst.at[slot], recvs.at[slot]).wait)

    relay_slot, rest_slot = 2 * c, 2 - 2 * c
    has_rest = z + 2 * c >= 2

    def spread(src, dst, sends, recvs):
        send(z + c < groups, src, dst.at[0], sends.at[0], recvs.at[0], (z + c, 1 - c, h))
        send(z + 1 + c < groups, src, dst.at[2], sends.at[1], recvs.at[2], (z + 1 + c, 1 - c, h))

    def gather(dst, sends, recvs):
        arrived(has_relay, dst, relay_slot, recvs)
        send(has_relay, dst.at[relay_slot], dst.at[1], sends.at[2], recvs.at[1], other)

    def gathered(dst, recvs):
        arrived(has_rest, dst, rest_slot, recvs)
        arrived(has_relay, dst, 1, recvs)

    for j in range(REACH):
        there = block + j + 1 < blocks
        send(there, seg, docs.at[j], doc_send.at[j], doc_recv.at[j], (*place(block + j + 1), h))
    spread(state, states, state_send, state_recv)
    loads[6].wait()
    spread(sk, keys, key_send, key_recv)

    loads[3].wait()
    at_t = lax.broadcasted_iota(jnp.int32, (tokens, tokens), 0)
    at_s = lax.broadcasted_iota(jnp.int32, (tokens, tokens), 1)
    own_seen = (at_t >= at_s) & (doc_col == doc_row)
    for cols in head_cols:
        intra = jnp.where(own_seen, matmul_nt(q[:, cols], k[:, cols]), 0.0).astype(BF16)
        mixed[:, cols] = matmul(intra, v[:, cols])
    loads[4].wait()
    loads[5].wait()
    for i, cols in enumerate(head_cols):
        gates[:, cols] = jax.nn.sigmoid(g[:, cols].astype(F32)) * gain[i : i + 1].astype(F32)

    for j in range(REACH):
        arrived(block > j, docs, j, doc_recv)

    gather(states, state_send, state_recv)
    gathered(states, state_recv)
    for cols in head_cols:
        q_f32 = q[:, cols].astype(F32)
        carried = None
        for j in range(REACH):
            last = docs[j].astype(F32)[:, tokens - 1 :]
            part = matmul(jnp.where(doc_col == last, q_f32, 0.0).astype(BF16), states[j, cols, :])
            carried = part if carried is None else carried + part
        mixed[:, cols] += carried

    square = mixed[...] * mixed[...]
    own_row[...] = matmul_nt(jnp.ones((8, heads * DH), BF16), square.astype(BF16))[:1]

    for d in range(1, y_chips):
        remote(own_row, rows_y.at[y], y_send, y_recv, (z, c, column_head(d))).start()
    rows_y[y] = own_row[...]
    mid[...] = (mixed[...] * gates[...]).astype(BF16)
    spread(mid, mids, mid_send, mid_recv)

    loads[7].wait()
    gather(keys, key_send, key_recv)
    gathered(keys, key_recv)
    scale = 1.0 / math.sqrt(DH)
    for i, cols in enumerate(head_cols):
        query = sq[:, cols]
        parts = [jnp.where(own_seen, matmul_nt(query, sk[:, cols]) * scale, -jnp.inf)]
        for j in range(REACH):
            seen = doc_col == docs[j].astype(F32)
            parts.append(jnp.where(seen, matmul_nt(query, keys[j, :, cols]) * scale, -jnp.inf))
        top = jnp.maximum(jnp.maximum(parts[0], parts[1]), jnp.maximum(parts[2], parts[3]))
        top = jnp.max(top, axis=1, keepdims=True)
        parts = [jnp.exp(part - top) for part in parts]
        total = jnp.sum(parts[0] + parts[1] + parts[2] + parts[3], axis=1, keepdims=True)
        for j, part in enumerate(parts):
            weights[i, j] = part / total

    if y_chips > 1:
        span = pl.ds(0, y_chips - 1)
        pltpu.make_async_copy(rows_y.at[span], rows_y.at[span], y_recv).wait()
    column_row = rows_x.at[0, x]
    column_row[...] = jnp.sum(rows_y[...], axis=0)
    for j in range(REACH + 1):

        @pl.when(block + j < blocks)
        def _(j=j):
            for d in range(0 if j else 1, x_chips):
                device = (*place(block + j), row_head(d))
                remote(column_row, rows_x.at[j, x], x_send.at[j], x_recv.at[j], device).start()

    gather(mids, mid_send, mid_recv)

    def x_span(j):
        return rows_x.at[j, pl.ds(0, x_chips if j else x_chips - 1)]

    def inverse_norm(j):
        pl.when(block >= j)(pltpu.make_async_copy(x_span(j), x_span(j), x_recv.at[j]).wait)
        return lax.rsqrt(jnp.sum(rows_x[j], axis=0) / total_columns + 1e-05)

    inverse = inverse_norm(0)
    inverse_col = column(inverse)
    for cols in head_cols:
        lin_out[:, cols] = (mixed[:, cols] * gates[:, cols] * inverse_col).astype(BF16)

    gathered(mids, mid_recv)
    inverses = [inverse] + [inverse_norm(j + 1) for j in range(REACH)]
    for i, cols in enumerate(head_cols):
        result = matmul((weights[i, 0] * inverses[0]).astype(BF16), mid[:, cols])
        for j in range(REACH):
            result += matmul((weights[i, j + 1] * inverses[j + 1]).astype(BF16), mids[j, :, cols])
        att_out[:, cols] = result.astype(BF16)

    for condition, copy in waits:
        pl.when(condition)(copy.wait_send)
    if y_chips > 1:
        pltpu.make_async_copy(rows_y.at[span], rows_y.at[span], y_send).wait()
    for j in range(REACH + 1):
        pl.when(block + j < blocks)(pltpu.make_async_copy(x_span(j), x_span(j), x_send.at[j]).wait)


def per_device(mesh, *args):
    q, k, v, g, gain, seg, sq, sk = args
    tokens, columns = q.shape
    groups = mesh.shape["outer"]
    x_chips = min(X_CHIPS, mesh.shape["heads"])
    y_chips = mesh.shape["heads"] // x_chips
    total_columns = columns * mesh.shape["heads"]
    seg = seg.reshape(1, tokens)
    gain = gain.reshape(columns // DH, DH)
    dma = pltpu.SemaphoreType.DMA
    block = (tokens, columns)
    stacked = (columns, DH)
    return pl.pallas_call(
        functools.partial(kernel, groups, x_chips, y_chips, total_columns),
        out_shape=(jax.ShapeDtypeStruct(block, BF16), jax.ShapeDtypeStruct(block, BF16)),
        in_specs=[pl.BlockSpec(memory_space=pl.ANY)] * 8,
        out_specs=(pl.BlockSpec(memory_space=pltpu.VMEM), pl.BlockSpec(memory_space=pltpu.VMEM)),
        scratch_shapes=[
            pltpu.VMEM(block, BF16), pltpu.VMEM(block, BF16), pltpu.VMEM(block, BF16), pltpu.VMEM(block, BF16),
            pltpu.VMEM((columns // DH, DH), BF16), pltpu.VMEM((1, tokens), jnp.int32),
            pltpu.VMEM(block, BF16), pltpu.VMEM(block, BF16),
            pltpu.VMEM((REACH, 1, tokens), jnp.int32),
            pltpu.VMEM(stacked, BF16), pltpu.VMEM((REACH,) + stacked, BF16),
            pltpu.VMEM((REACH,) + block, BF16),
            pltpu.VMEM(block, BF16), pltpu.VMEM((REACH,) + block, BF16),
            pltpu.VMEM((1, tokens), F32),
            pltpu.VMEM((y_chips, 1, tokens), F32),
            pltpu.VMEM((REACH + 1, x_chips, 1, tokens), F32),
            pltpu.VMEM(block, F32), pltpu.VMEM(block, F32),
            pltpu.VMEM((columns // DH, REACH + 1, tokens, tokens), F32),
            dma((8,)),
            dma((REACH,)), dma((REACH,)), dma((3,)), dma((REACH,)), dma((3,)), dma((REACH,)), dma((3,)), dma((REACH,)),
            dma, dma, dma((REACH + 1,)), dma((REACH + 1,)),
        ],
        compiler_params=pltpu.CompilerParams(collective_id=0, has_side_effects=True),
    )(q, k, v, g, gain, seg, sq, sk)


def solution(mesh):
    block = P(("outer", "inner"), "heads")
    return jax.shard_map(
        functools.partial(per_device, mesh),
        mesh=mesh,
        in_specs=(block, block, block, block, P("heads"), P(("outer", "inner")), block, block),
        out_specs=(block, block),
        check_vma=False,
    )
```

```python
import functools
import math

import jax
import jax.numpy as jnp
from jax import lax
from jax.experimental import pallas as pl
from jax.experimental.pallas import tpu as pltpu
from jax.sharding import PartitionSpec as P

DH = 128
X_CHIPS = 4
REACH = 3
MESH = pl.DeviceIdType.MESH
F32 = jnp.float32
BF16 = jnp.bfloat16


def matmul(a, b):
    return jnp.dot(a, b, preferred_element_type=F32)


def matmul_nt(a, b):
    return lax.dot_general(a, b, (((1,), (1,)), ((), ())), preferred_element_type=F32)


def matmul_tn(a, b):
    return lax.dot_general(a, b, (((0,), (0,)), ((), ())), preferred_element_type=F32)


def column(row):
    n = row.shape[1]
    return jnp.transpose(jnp.broadcast_to(row, (n, n)))


def kernel(
    groups, x_chips, y_chips, total_columns,
    q_in, k_in, v_in, g_in, gain_in, seg_in, sq_in, sk_in,
    out,
    q, k, v, g, gain, seg, sq, sk,
    state, states, keys, mid, mids, own_row, rows_y, rows_x,
    gates, mixed, weights,
    load_sem, state_send, state_recv, key_send, key_recv, mid_send, mid_recv,
    y_send, y_recv, x_send, x_recv, hop_sem, ring_sem, later_sem,
):
    z = lax.axis_index("outer")
    c = lax.axis_index("inner")
    h = lax.axis_index("heads")
    y, x = h // x_chips, h % x_chips
    block = 2 * z + c
    blocks = 2 * groups
    tokens = q.shape[0]
    heads = q.shape[1] // DH
    head_cols = [slice(i * DH, (i + 1) * DH) for i in range(heads)]

    def place(n):
        return n // 2, n % 2

    def row_head(d):
        return y * x_chips + lax.rem(x + d, x_chips)

    def column_head(d):
        return lax.rem(y + d, y_chips) * x_chips + x

    other = (z, 1 - c, h)
    has_relay = z >= 1
    barrier = pltpu.get_barrier_semaphore()

    def signal(sem, device):
        pl.semaphore_signal(sem, inc=1, device_id=device, device_id_type=MESH)

    def signal_if(condition, sem, device):
        pl.when(condition)(lambda: signal(sem, device))

    loads = [
        pltpu.make_async_copy(a, b, load_sem.at[i])
        for i, (a, b) in enumerate(
            ((seg_in, seg), (k_in, k), (v_in, v), (q_in, q), (gain_in, gain), (g_in, g), (sk_in, sk), (sq_in, sq))
        )
    ]
    for copy in loads[:3]:
        copy.start()

    near_blocks = [
        (block >= 1, block - 1), (block >= 2, block - 2), (block + 1 < blocks, block + 1), (block + 2 < blocks, block + 2),
        ((c == 1) & (block >= 3), block - 3), ((c == 0) & (block + 3 < blocks), block + 3),
    ]
    near_heads = [row_head(d) for d in range(1, x_chips)] + [column_head(d) for d in (1, y_chips - 1, 2, y_chips - 2)]
    for condition, n in near_blocks:
        signal_if(condition, barrier, (*place(n), h))
    for head in near_heads:
        signal(barrier, (z, c, head))
    for copy in loads[3:]:
        copy.start()

    columns = heads * DH
    for j in range(1, REACH + 1):

        @pl.when(block < j)
        def _(j=j):
            states[j - 1, :columns] = jnp.zeros((columns, DH), BF16)
            states[j - 1, columns:] = jnp.full((states.shape[1] - columns, DH), -1.0, BF16)
            keys[j - 1] = jnp.zeros(keys.shape[1:], BF16)
            mids[j - 1] = jnp.zeros(mids.shape[1:], BF16)
            rows_x[j] = jnp.zeros(rows_x.shape[1:], F32)

    for copy in loads[:3]:
        copy.wait()
    doc_row = seg[...].astype(F32)
    doc_col = column(doc_row)
    kept = doc_col == doc_row[:, tokens - 1 :]
    for cols in head_cols:
        masked = jnp.where(kept, k[:, cols].astype(F32), 0.0).astype(BF16)
        state[cols, :] = matmul_tn(masked, v[:, cols]).astype(BF16)

    state[columns:, :] = jnp.broadcast_to(doc_row, (state.shape[0] - columns, tokens)).astype(BF16)

    def count(*conditions):
        return sum(condition.astype(jnp.int32) for condition in conditions)

    pl.semaphore_wait(barrier, len(near_heads) + count(*[condition for condition, _ in near_blocks]))

    middle = (c == 0) & (z >= 1) & (z + 1 < groups)
    signal_if(middle, hop_sem, (z - 1, 1, h))
    signal_if(middle, hop_sem, (z + 1, 0, h))

    waits = []

    def remote(src, dst, send_sem, recv_sem, device):
        return pltpu.make_async_remote_copy(
            src_ref=src, dst_ref=dst, send_sem=send_sem, recv_sem=recv_sem, device_id=device, device_id_type=MESH
        )

    def send(condition, *args):
        copy = remote(*args)
        pl.when(condition)(copy.start)
        waits.append((condition, copy))

    def arrived(condition, dst, slot, recvs):
        pl.when(condition)(pltpu.make_async_copy(dst.at[slot], dst.at[slot], recvs.at[slot]).wait)

    relay_slot, rest_slot = 2 * c, 2 - 2 * c
    has_rest = z + 2 * c >= 2

    def send_near(src, dst, sends, recvs):
        send(z + c < groups, src, dst.at[0], sends.at[0], recvs.at[0], (z + c, 1 - c, h))

    def send_far(src, dst, sends, recvs, condition=True):
        there = condition & (z + 1 + c < groups)
        send(there, src, dst.at[2], sends.at[1], recvs.at[2], (z + 1 + c, 1 - c, h))

    def spread(src, dst, sends, recvs):
        send_near(src, dst, sends, recvs)
        send_far(src, dst, sends, recvs)

    def gather(dst, sends, recvs):
        arrived(has_relay, dst, relay_slot, recvs)
        send(has_relay, dst.at[relay_slot], dst.at[1], sends.at[2], recvs.at[1], other)

    def gathered(dst, recvs):
        arrived(has_rest, dst, rest_slot, recvs)
        arrived(has_relay, dst, 1, recvs)

    send_near(state, states, state_send, state_recv)
    send_far(state, states, state_send, state_recv, c == 0)
    for d in (2, y_chips - 2):
        signal(ring_sem, (z, c, column_head(d)))
    for j in range(1, REACH + 1):
        signal_if((block >= j) & ((c == 1) if j == REACH else True), later_sem, (*place(block - j), h))

    loads[3].wait()
    at_t = lax.broadcasted_iota(jnp.int32, (tokens, tokens), 0)
    at_s = lax.broadcasted_iota(jnp.int32, (tokens, tokens), 1)
    own_seen = (at_t >= at_s) & (doc_col == doc_row)
    for cols in head_cols:
        intra = jnp.where(own_seen, matmul_nt(q[:, cols], k[:, cols]), 0.0).astype(BF16)
        mixed[:, cols] = matmul(intra, v[:, cols])
    loads[4].wait()
    loads[5].wait()
    for i, cols in enumerate(head_cols):
        gates[:, cols] = jax.nn.sigmoid(g[:, cols].astype(F32)) * gain[i : i + 1].astype(F32)

    pl.when(((c == 0) & (z >= 2)) | ((c == 1) & (z + 2 < groups)))(lambda: pl.semaphore_wait(hop_sem, 1))
    send_far(state, states, state_send, state_recv, c == 1)
    signal_if((c == 0) & (z >= 2), later_sem, (z - 2, 1, h))
    loads[6].wait()
    spread(sk, keys, key_send, key_recv)

    gather(states, state_send, state_recv)
    gathered(states, state_recv)
    doc_rows = [states[j, columns : columns + 1, :].astype(F32) for j in range(REACH)]
    for cols in head_cols:
        q_f32 = q[:, cols].astype(F32)
        carried = None
        for j in range(REACH):
            last = doc_rows[j][:, tokens - 1 :]
            part = matmul(jnp.where(doc_col == last, q_f32, 0.0).astype(BF16), states[j, cols, :])
            carried = part if carried is None else carried + part
        mixed[:, cols] += carried

    square = mixed[...] * mixed[...]
    own_row[...] = matmul_nt(jnp.ones((8, heads * DH), BF16), square.astype(BF16))[:1]

    pl.semaphore_wait(ring_sem, 2)
    for d in range(1, y_chips):
        remote(own_row, rows_y.at[y], y_send, y_recv, (z, c, column_head(d))).start()
    rows_y[y] = own_row[...]
    mid[...] = (mixed[...] * gates[...]).astype(BF16)
    spread(mid, mids, mid_send, mid_recv)
    gather(keys, key_send, key_recv)

    y_span = rows_y.at[pl.ds(0, y_chips - 1)]
    pltpu.make_async_copy(y_span, y_span, y_recv).wait()
    column_row = rows_x.at[0, x]
    column_row[...] = jnp.sum(rows_y[...], axis=0)
    after = jnp.minimum(REACH, blocks - 1 - block)
    pl.when(after > 0)(lambda: pl.semaphore_wait(later_sem, after))
    for j in range(REACH + 1):

        @pl.when(block + j < blocks)
        def _(j=j):
            for d in range(0 if j else 1, x_chips):
                device = (*place(block + j), row_head(d))
                remote(column_row, rows_x.at[j, x], x_send.at[j], x_recv.at[j], device).start()

    gather(mids, mid_send, mid_recv)

    loads[7].wait()
    gathered(keys, key_recv)
    scale = 1.0 / math.sqrt(DH)
    for i, cols in enumerate(head_cols):
        query = sq[:, cols]
        parts = [jnp.where(own_seen, matmul_nt(query, sk[:, cols]) * scale, -jnp.inf)]
        for j in range(REACH):
            seen = doc_col == doc_rows[j]
            parts.append(jnp.where(seen, matmul_nt(query, keys[j, :, cols]) * scale, -jnp.inf))
        top = jnp.maximum(jnp.maximum(parts[0], parts[1]), jnp.maximum(parts[2], parts[3]))
        top = jnp.max(top, axis=1, keepdims=True)
        parts = [jnp.exp(part - top) for part in parts]
        total = jnp.sum(parts[0] + parts[1] + parts[2] + parts[3], axis=1, keepdims=True)
        for j, part in enumerate(parts):
            weights[i, j] = part / total

    def x_span(j):
        return rows_x.at[j, pl.ds(0, x_chips if j else x_chips - 1)]

    def inverse_norm(j):
        pl.when(block >= j)(pltpu.make_async_copy(x_span(j), x_span(j), x_recv.at[j]).wait)
        return lax.rsqrt(jnp.sum(rows_x[j], axis=0) / total_columns + 1e-05)

    inverse = inverse_norm(0)
    inverse_col = column(inverse)
    for cols in head_cols:
        out[0, :, cols] = (mixed[:, cols] * gates[:, cols] * inverse_col).astype(BF16)

    gathered(mids, mid_recv)
    inverses = [inverse] + [inverse_norm(j + 1) for j in range(REACH)]
    for i, cols in enumerate(head_cols):
        result = matmul((weights[i, 0] * inverses[0]).astype(BF16), mid[:, cols])
        for j in range(REACH):
            result += matmul((weights[i, j + 1] * inverses[j + 1]).astype(BF16), mids[j, :, cols])
        out[1, :, cols] = result.astype(BF16)

    for condition, copy in waits:
        pl.when(condition)(copy.wait_send)
    pltpu.make_async_copy(y_span, y_span, y_send).wait()
    for j in range(REACH + 1):
        pl.when(block + j < blocks)(pltpu.make_async_copy(x_span(j), x_span(j), x_send.at[j]).wait)


def per_device(mesh, *args):
    q, k, v, g, gain, seg, sq, sk = args
    tokens, columns = q.shape
    groups = mesh.shape["outer"]
    x_chips = min(X_CHIPS, mesh.shape["heads"])
    y_chips = mesh.shape["heads"] // x_chips
    total_columns = columns * mesh.shape["heads"]
    seg = seg.reshape(1, tokens)
    gain = gain.reshape(columns // DH, DH)
    dma = pltpu.SemaphoreType.DMA
    regular = pltpu.SemaphoreType.REGULAR
    block = (tokens, columns)
    stacked = (columns + 16, DH)
    outs = pl.pallas_call(
        functools.partial(kernel, groups, x_chips, y_chips, total_columns),
        out_shape=pltpu.VMEM((2,) + block, BF16),
        in_specs=[pl.BlockSpec(memory_space=pl.ANY)] * 8,
        out_specs=pl.BlockSpec(memory_space=pltpu.VMEM),
        scratch_shapes=[
            pltpu.VMEM(block, BF16), pltpu.VMEM(block, BF16), pltpu.VMEM(block, BF16), pltpu.VMEM(block, BF16),
            pltpu.VMEM((columns // DH, DH), BF16), pltpu.VMEM((1, tokens), jnp.int32),
            pltpu.VMEM(block, BF16), pltpu.VMEM(block, BF16),
            pltpu.VMEM(stacked, BF16), pltpu.VMEM((REACH,) + stacked, BF16),
            pltpu.VMEM((REACH,) + block, BF16),
            pltpu.VMEM(block, BF16), pltpu.VMEM((REACH,) + block, BF16),
            pltpu.VMEM((1, tokens), F32),
            pltpu.VMEM((y_chips, 1, tokens), F32),
            pltpu.VMEM((REACH + 1, x_chips, 1, tokens), F32),
            pltpu.VMEM(block, F32), pltpu.VMEM(block, F32),
            pltpu.VMEM((columns // DH, REACH + 1, tokens, tokens), F32),
            dma((8,)),
            dma((3,)), dma((REACH,)), dma((3,)), dma((REACH,)), dma((3,)), dma((REACH,)),
            dma, dma, dma((REACH + 1,)), dma((REACH + 1,)),
            regular, regular, regular,
        ],
        compiler_params=pltpu.CompilerParams(collective_id=0, has_side_effects=True),
    )(q, k, v, g, gain, seg, sq, sk)
    return outs[0], outs[1]


def solution(mesh):
    block = P(("outer", "inner"), "heads")
    return jax.shard_map(
        functools.partial(per_device, mesh),
        mesh=mesh,
        in_specs=(block, block, block, block, P("heads"), P(("outer", "inner")), block, block),
        out_specs=(block, block),
        check_vma=False,
    )
```

```python
import functools
import math

import jax
import jax.numpy as jnp
from jax import lax
from jax.experimental import pallas as pl
from jax.experimental.pallas import tpu as pltpu
from jax.sharding import PartitionSpec as P

DH = 128
X_CHIPS = 4
REACH = 3
MESH = pl.DeviceIdType.MESH
F32 = jnp.float32
BF16 = jnp.bfloat16


def matmul(a, b):
    return jnp.dot(a, b, preferred_element_type=F32)


def matmul_nt(a, b):
    return lax.dot_general(a, b, (((1,), (1,)), ((), ())), preferred_element_type=F32)


def matmul_tn(a, b):
    return lax.dot_general(a, b, (((0,), (0,)), ((), ())), preferred_element_type=F32)


def column(row):
    n = row.shape[1]
    return jnp.transpose(jnp.broadcast_to(row, (n, n)))


def kernel(
    groups, x_chips, y_chips, total_columns,
    q_in, k_in, v_in, g_in, gain_in, seg_in, sq_in, sk_in,
    out,
    q, k, v, g, gain, seg, sq, sk,
    state, states, keys, mid, mids, own_row, rows_y, rows_x,
    gates, mixed, weights,
    load_sem, state_send, state_recv, key_send, key_recv, mid_send, mid_recv,
    y_send, y_recv, x_send, x_recv, hop_sem, ring_sem, later_sem, go_sem,
):
    z = lax.axis_index("outer")
    c = lax.axis_index("inner")
    h = lax.axis_index("heads")
    y, x = h // x_chips, h % x_chips
    block = 2 * z + c
    blocks = 2 * groups
    tokens = q.shape[0]
    heads = q.shape[1] // DH
    head_cols = [slice(i * DH, (i + 1) * DH) for i in range(heads)]

    def place(n):
        return n // 2, n % 2

    def row_head(d):
        return y * x_chips + lax.rem(x + d, x_chips)

    def column_head(d):
        return lax.rem(y + d, y_chips) * x_chips + x

    other = (z, 1 - c, h)
    has_relay = z >= 1
    barrier = pltpu.get_barrier_semaphore()

    def signal(sem, device):
        pl.semaphore_signal(sem, inc=1, device_id=device, device_id_type=MESH)

    def signal_if(condition, sem, device):
        pl.when(condition)(lambda: signal(sem, device))

    loads = [
        pltpu.make_async_copy(a, b, load_sem.at[i])
        for i, (a, b) in enumerate(
            ((seg_in, seg), (k_in, k), (v_in, v), (q_in, q), (gain_in, gain), (g_in, g), (sk_in, sk), (sq_in, sq))
        )
    ]
    for copy in loads[:3]:
        copy.start()

    first = block == 0
    earlier = [(True, block - 1), (True, block - 2), (c == 1, block - 3)]
    later = [(True, block + 1), (True, block + 2), (c == 0, block + 3)]
    reached = [(near & (n >= 1), n) for near, n in earlier] + [(near & (n < blocks), n) for near, n in later]
    heard = [near & (n >= 0) for near, n in earlier] + [near & (n < blocks) & (block > 0) for near, n in later]
    near_heads = [row_head(d) for d in range(1, x_chips)] + [column_head(d) for d in (1, y_chips - 1, 2, y_chips - 2)]
    for condition, n in reached:
        signal_if(condition, barrier, (*place(n), h))
    for head in near_heads:
        signal(barrier, (z, c, head))
    far_heads = [column_head(d) for d in range(3, y_chips - 2)]
    for head in far_heads:
        signal_if(first, barrier, (z, c, head))
    for copy in loads[3:]:
        copy.start()

    columns = heads * DH
    for j in range(1, REACH + 1):

        @pl.when(block < j)
        def _(j=j):
            states[j - 1, :columns] = jnp.zeros((columns, DH), BF16)
            states[j - 1, columns:] = jnp.full((states.shape[1] - columns, DH), -1.0, BF16)
            keys[j - 1] = jnp.zeros(keys.shape[1:], BF16)
            mids[j - 1] = jnp.zeros(mids.shape[1:], BF16)
            rows_x[j] = jnp.zeros(rows_x.shape[1:], F32)

    for copy in loads[:3]:
        copy.wait()
    doc_row = seg[...].astype(F32)
    doc_col = column(doc_row)
    kept = doc_col == doc_row[:, tokens - 1 :]
    for cols in head_cols:
        masked = jnp.where(kept, k[:, cols].astype(F32), 0.0).astype(BF16)
        state[cols, :] = matmul_tn(masked, v[:, cols]).astype(BF16)

    state[columns:, :] = jnp.broadcast_to(doc_row, (state.shape[0] - columns, tokens)).astype(BF16)

    def count(*conditions):
        return sum(condition.astype(jnp.int32) for condition in conditions)

    pl.when(block > 0)(lambda: pl.semaphore_wait(barrier, len(near_heads) + count(*heard)))
    pl.when(first)(lambda: pl.semaphore_wait(go_sem, 1))
    signal_if(block == 1, go_sem, other)

    middle = (c == 0) & (z >= 1) & (z + 1 < groups)
    signal_if(middle, hop_sem, (z - 1, 1, h))
    signal_if(middle, hop_sem, (z + 1, 0, h))

    waits = []

    def remote(src, dst, send_sem, recv_sem, device):
        return pltpu.make_async_remote_copy(
            src_ref=src, dst_ref=dst, send_sem=send_sem, recv_sem=recv_sem, device_id=device, device_id_type=MESH
        )

    def send(condition, *args):
        copy = remote(*args)
        pl.when(condition)(copy.start)
        waits.append((condition, copy))

    def arrived(condition, dst, slot, recvs):
        pl.when(condition)(pltpu.make_async_copy(dst.at[slot], dst.at[slot], recvs.at[slot]).wait)

    relay_slot, rest_slot = 2 * c, 2 - 2 * c
    has_rest = z + 2 * c >= 2

    def send_near(src, dst, sends, recvs):
        send(z + c < groups, src, dst.at[0], sends.at[0], recvs.at[0], (z + c, 1 - c, h))

    def send_far(src, dst, sends, recvs, condition=True):
        there = condition & (z + 1 + c < groups)
        send(there, src, dst.at[2], sends.at[1], recvs.at[2], (z + 1 + c, 1 - c, h))

    def spread(src, dst, sends, recvs):
        send_near(src, dst, sends, recvs)
        send_far(src, dst, sends, recvs)

    def gather(dst, sends, recvs):
        arrived(has_relay, dst, relay_slot, recvs)
        send(has_relay, dst.at[relay_slot], dst.at[1], sends.at[2], recvs.at[1], other)

    def gathered(dst, recvs):
        arrived(has_rest, dst, rest_slot, recvs)
        arrived(has_relay, dst, 1, recvs)

    send_near(state, states, state_send, state_recv)
    send_far(state, states, state_send, state_recv, c == 0)
    for d in (2, y_chips - 2):
        signal_if(block > 0, ring_sem, (z, c, column_head(d)))
    for j in range(1, REACH + 1):
        signal_if((block >= j) & ((c == 1) if j == REACH else True), later_sem, (*place(block - j), h))

    loads[3].wait()
    at_t = lax.broadcasted_iota(jnp.int32, (tokens, tokens), 0)
    at_s = lax.broadcasted_iota(jnp.int32, (tokens, tokens), 1)
    own_seen = (at_t >= at_s) & (doc_col == doc_row)
    for cols in head_cols:
        intra = jnp.where(own_seen, matmul_nt(q[:, cols], k[:, cols]), 0.0).astype(BF16)
        mixed[:, cols] = matmul(intra, v[:, cols])
    loads[4].wait()
    loads[5].wait()
    for i, cols in enumerate(head_cols):
        gates[:, cols] = jax.nn.sigmoid(g[:, cols].astype(F32)) * gain[i : i + 1].astype(F32)

    pl.when(((c == 0) & (z >= 2)) | ((c == 1) & (z + 2 < groups)))(lambda: pl.semaphore_wait(hop_sem, 1))
    send_far(state, states, state_send, state_recv, c == 1)
    signal_if((c == 0) & (z >= 2), later_sem, (z - 2, 1, h))
    gather(states, state_send, state_recv)
    gathered(states, state_recv)
    loads[6].wait()
    spread(sk, keys, key_send, key_recv)
    doc_rows = [states[j, columns : columns + 1, :].astype(F32) for j in range(REACH)]
    for cols in head_cols:
        q_f32 = q[:, cols].astype(F32)
        carried = None
        for j in range(REACH):
            last = doc_rows[j][:, tokens - 1 :]
            part = matmul(jnp.where(doc_col == last, q_f32, 0.0).astype(BF16), states[j, cols, :])
            carried = part if carried is None else carried + part
        mixed[:, cols] += carried

    square = mixed[...] * mixed[...]
    own_row[...] = matmul_nt(jnp.ones((8, heads * DH), BF16), square.astype(BF16))[:1]

    pl.when(block > 0)(lambda: pl.semaphore_wait(ring_sem, 2))
    pl.when(first)(lambda: pl.semaphore_wait(barrier, len(near_heads) + len(far_heads)))
    for d in range(1, y_chips):
        remote(own_row, rows_y.at[y], y_send, y_recv, (z, c, column_head(d))).start()
    rows_y[y] = own_row[...]
    mid[...] = (mixed[...] * gates[...]).astype(BF16)
    spread(mid, mids, mid_send, mid_recv)
    gather(keys, key_send, key_recv)

    y_span = rows_y.at[pl.ds(0, y_chips - 1)]
    pltpu.make_async_copy(y_span, y_span, y_recv).wait()
    column_row = rows_x.at[0, x]
    column_row[...] = jnp.sum(rows_y[...], axis=0)
    after = jnp.minimum(REACH, blocks - 1 - block)
    pl.when(after > 0)(lambda: pl.semaphore_wait(later_sem, after))
    for j in range(REACH + 1):

        @pl.when(block + j < blocks)
        def _(j=j):
            for d in range(0 if j else 1, x_chips):
                device = (*place(block + j), row_head(d))
                remote(column_row, rows_x.at[j, x], x_send.at[j], x_recv.at[j], device).start()

    gather(mids, mid_send, mid_recv)

    loads[7].wait()
    gathered(keys, key_recv)
    scale = 1.0 / math.sqrt(DH)
    for i, cols in enumerate(head_cols):
        query = sq[:, cols]
        parts = [jnp.where(own_seen, matmul_nt(query, sk[:, cols]) * scale, -jnp.inf)]
        for j in range(REACH):
            seen = doc_col == doc_rows[j]
            parts.append(jnp.where(seen, matmul_nt(query, keys[j, :, cols]) * scale, -jnp.inf))
        top = jnp.maximum(jnp.maximum(parts[0], parts[1]), jnp.maximum(parts[2], parts[3]))
        top = jnp.max(top, axis=1, keepdims=True)
        parts = [jnp.exp(part - top) for part in parts]
        total = jnp.sum(parts[0] + parts[1] + parts[2] + parts[3], axis=1, keepdims=True)
        for j, part in enumerate(parts):
            weights[i, j] = part / total

    def x_span(j):
        return rows_x.at[j, pl.ds(0, x_chips if j else x_chips - 1)]

    def inverse_norm(j):
        pl.when(block >= j)(pltpu.make_async_copy(x_span(j), x_span(j), x_recv.at[j]).wait)
        return lax.rsqrt(jnp.sum(rows_x[j], axis=0) / total_columns + 1e-05)

    inverse = inverse_norm(0)
    inverse_col = column(inverse)
    for cols in head_cols:
        out[0, :, cols] = (mixed[:, cols] * gates[:, cols] * inverse_col).astype(BF16)

    def attend(j, values):
        norm = inverse if j == 0 else inverse_norm(j)
        return [matmul((weights[i, j] * norm).astype(BF16), values[:, cols]) for i, cols in enumerate(head_cols)]

    results = attend(0, mid)
    gathered(mids, mid_recv)
    for j in range(REACH, 0, -1):
        results = [result + part for result, part in zip(results, attend(j, mids.at[j - 1]))]
    for result, cols in zip(results, head_cols):
        out[1, :, cols] = result.astype(BF16)

    for condition, copy in waits:
        pl.when(condition)(copy.wait_send)
    pltpu.make_async_copy(y_span, y_span, y_send).wait()
    for j in range(REACH + 1):
        pl.when(block + j < blocks)(pltpu.make_async_copy(x_span(j), x_span(j), x_send.at[j]).wait)


def per_device(mesh, *args):
    q, k, v, g, gain, seg, sq, sk = args
    tokens, columns = q.shape
    groups = mesh.shape["outer"]
    x_chips = min(X_CHIPS, mesh.shape["heads"])
    y_chips = mesh.shape["heads"] // x_chips
    total_columns = columns * mesh.shape["heads"]
    seg = seg.reshape(1, tokens)
    gain = gain.reshape(columns // DH, DH)
    dma = pltpu.SemaphoreType.DMA
    regular = pltpu.SemaphoreType.REGULAR
    block = (tokens, columns)
    stacked = (columns + 16, DH)
    outs = pl.pallas_call(
        functools.partial(kernel, groups, x_chips, y_chips, total_columns),
        out_shape=pltpu.VMEM((2,) + block, BF16),
        in_specs=[pl.BlockSpec(memory_space=pl.ANY)] * 8,
        out_specs=pl.BlockSpec(memory_space=pltpu.VMEM),
        scratch_shapes=[
            pltpu.VMEM(block, BF16), pltpu.VMEM(block, BF16), pltpu.VMEM(block, BF16), pltpu.VMEM(block, BF16),
            pltpu.VMEM((columns // DH, DH), BF16), pltpu.VMEM((1, tokens), jnp.int32),
            pltpu.VMEM(block, BF16), pltpu.VMEM(block, BF16),
            pltpu.VMEM(stacked, BF16), pltpu.VMEM((REACH,) + stacked, BF16),
            pltpu.VMEM((REACH,) + block, BF16),
            pltpu.VMEM(block, BF16), pltpu.VMEM((REACH,) + block, BF16),
            pltpu.VMEM((1, tokens), F32),
            pltpu.VMEM((y_chips, 1, tokens), F32),
            pltpu.VMEM((REACH + 1, x_chips, 1, tokens), F32),
            pltpu.VMEM(block, F32), pltpu.VMEM(block, F32),
            pltpu.VMEM((columns // DH, REACH + 1, tokens, tokens), F32),
            dma((8,)),
            dma((3,)), dma((REACH,)), dma((3,)), dma((REACH,)), dma((3,)), dma((REACH,)),
            dma, dma, dma((REACH + 1,)), dma((REACH + 1,)),
            regular, regular, regular, regular,
        ],
        compiler_params=pltpu.CompilerParams(collective_id=0, has_side_effects=True),
    )(q, k, v, g, gain, seg, sq, sk)
    return outs[0], outs[1]


def solution(mesh):
    block = P(("outer", "inner"), "heads")
    return jax.shard_map(
        functools.partial(per_device, mesh),
        mesh=mesh,
        in_specs=(block, block, block, block, P("heads"), P(("outer", "inner")), block, block),
        out_specs=(block, block),
        check_vma=False,
    )
```

```python
import functools
import math

import jax
import jax.numpy as jnp
from jax import lax
from jax.experimental import pallas as pl
from jax.experimental.pallas import tpu as pltpu
from jax.sharding import PartitionSpec as P

DH = 128
X_CHIPS = 4
REACH = 3
MESH = pl.DeviceIdType.MESH
F32 = jnp.float32
BF16 = jnp.bfloat16


def matmul(a, b):
    return jnp.dot(a, b, preferred_element_type=F32)


def matmul_nt(a, b):
    return lax.dot_general(a, b, (((1,), (1,)), ((), ())), preferred_element_type=F32)


def matmul_tn(a, b):
    return lax.dot_general(a, b, (((0,), (0,)), ((), ())), preferred_element_type=F32)


def column(row):
    n = row.shape[1]
    return jnp.transpose(jnp.broadcast_to(row, (n, n)))


def kernel(
    groups, x_chips, y_chips, total_columns,
    q_in, k_in, v_in, g_in, gain_in, seg_in, sq_in, sk_in,
    out,
    q, k, v, g, gain, seg, sq, sk,
    state, states, keys, mid, mids, own_row, rows_y, rows_x,
    gates, mixed, weights,
    load_sem, state_send, state_recv, key_send, key_recv, mid_send, mid_recv,
    y_send, y_recv, x_send, x_recv, hop_sem, ring_sem, later_sem, go_sem,
):
    z = lax.axis_index("outer")
    c = lax.axis_index("inner")
    h = lax.axis_index("heads")
    y, x = h // x_chips, h % x_chips
    block = 2 * z + c
    blocks = 2 * groups
    tokens = q.shape[0]
    heads = q.shape[1] // DH
    head_cols = [slice(i * DH, (i + 1) * DH) for i in range(heads)]

    def place(n):
        return n // 2, n % 2

    def row_head(d):
        return y * x_chips + lax.rem(x + d, x_chips)

    def column_head(d):
        return lax.rem(y + d, y_chips) * x_chips + x

    other = (z, 1 - c, h)
    has_relay = z >= 1
    barrier = pltpu.get_barrier_semaphore()

    def signal(sem, device):
        pl.semaphore_signal(sem, inc=1, device_id=device, device_id_type=MESH)

    def signal_if(condition, sem, device):
        pl.when(condition)(lambda: signal(sem, device))

    loads = [
        pltpu.make_async_copy(a, b, load_sem.at[i])
        for i, (a, b) in enumerate(
            ((seg_in, seg), (k_in, k), (v_in, v), (q_in, q), (gain_in, gain), (g_in, g), (sk_in, sk), (sq_in, sq))
        )
    ]
    for copy in loads[:3]:
        copy.start()

    first = block == 0
    earlier = [(True, block - 1), (True, block - 2), (c == 1, block - 3)]
    later = [(True, block + 1), (True, block + 2), (c == 0, block + 3)]
    reached = [(near & (n >= 1), n) for near, n in earlier] + [(near & (n < blocks), n) for near, n in later]
    heard = [near & (n >= 0) for near, n in earlier] + [near & (n < blocks) & (block > 0) for near, n in later]
    near_heads = [row_head(d) for d in range(1, x_chips)] + [column_head(d) for d in (1, y_chips - 1, 2, y_chips - 2)]
    for condition, n in reached:
        signal_if(condition, barrier, (*place(n), h))
    for head in near_heads:
        signal(barrier, (z, c, head))
    far_heads = [column_head(d) for d in range(3, y_chips - 2)]
    for head in far_heads:
        signal_if(first, barrier, (z, c, head))
    for copy in loads[3:]:
        copy.start()

    columns = heads * DH
    for j in range(1, REACH + 1):

        @pl.when(block < j)
        def _(j=j):
            states[j - 1, :columns] = jnp.zeros((columns, DH), BF16)
            states[j - 1, columns:] = jnp.full((states.shape[1] - columns, DH), -1.0, BF16)
            keys[j - 1] = jnp.zeros(keys.shape[1:], BF16)
            mids[j - 1] = jnp.zeros(mids.shape[1:], BF16)
            rows_x[j] = jnp.zeros(rows_x.shape[1:], F32)

    for copy in loads[:3]:
        copy.wait()
    doc_row = seg[...].astype(F32)
    doc_col = column(doc_row)
    kept = doc_col == doc_row[:, tokens - 1 :]
    for cols in head_cols:
        masked = jnp.where(kept, k[:, cols].astype(F32), 0.0).astype(BF16)
        state[cols, :] = matmul_tn(masked, v[:, cols]).astype(BF16)

    state[columns:, :] = jnp.broadcast_to(doc_row, (state.shape[0] - columns, tokens)).astype(BF16)

    def count(*conditions):
        return sum(condition.astype(jnp.int32) for condition in conditions)

    pl.when(block > 0)(lambda: pl.semaphore_wait(barrier, len(near_heads) + count(*heard)))
    pl.when(first)(lambda: pl.semaphore_wait(go_sem, 1))
    signal_if(block == 1, go_sem, other)

    middle = (c == 0) & (z >= 1) & (z + 1 < groups)
    signal_if(middle, hop_sem, (z - 1, 1, h))
    signal_if(middle, hop_sem, (z + 1, 0, h))

    waits = []

    def remote(src, dst, send_sem, recv_sem, device):
        return pltpu.make_async_remote_copy(
            src_ref=src, dst_ref=dst, send_sem=send_sem, recv_sem=recv_sem, device_id=device, device_id_type=MESH
        )

    def send(condition, *args):
        copy = remote(*args)
        pl.when(condition)(copy.start)
        waits.append((condition, copy))

    def arrived(condition, dst, slot, recvs):
        pl.when(condition)(pltpu.make_async_copy(dst.at[slot], dst.at[slot], recvs.at[slot]).wait)

    relay_slot, rest_slot = 2 * c, 2 - 2 * c
    has_rest = z + 2 * c >= 2

    def send_near(src, dst, sends, recvs):
        send(z + c < groups, src, dst.at[0], sends.at[0], recvs.at[0], (z + c, 1 - c, h))

    def send_far(src, dst, sends, recvs, condition=True):
        there = condition & (z + 1 + c < groups)
        send(there, src, dst.at[2], sends.at[1], recvs.at[2], (z + 1 + c, 1 - c, h))

    def spread(src, dst, sends, recvs):
        send_near(src, dst, sends, recvs)
        send_far(src, dst, sends, recvs)

    def gather(dst, sends, recvs, condition=True):
        here = has_relay & condition
        arrived(here, dst, relay_slot, recvs)
        send(here, dst.at[relay_slot], dst.at[1], sends.at[2], recvs.at[1], other)

    def gathered(dst, recvs):
        arrived(has_rest, dst, rest_slot, recvs)
        arrived(has_relay, dst, 1, recvs)

    send_near(state, states, state_send, state_recv)
    send_far(state, states, state_send, state_recv, c == 0)
    for d in (2, y_chips - 2):
        signal_if(block > 0, ring_sem, (z, c, column_head(d)))
    for j in range(1, REACH + 1):
        signal_if((block >= j) & ((c == 1) if j == REACH else True), later_sem, (*place(block - j), h))

    loads[3].wait()
    at_t = lax.broadcasted_iota(jnp.int32, (tokens, tokens), 0)
    at_s = lax.broadcasted_iota(jnp.int32, (tokens, tokens), 1)
    own_seen = (at_t >= at_s) & (doc_col == doc_row)
    for cols in head_cols:
        intra = jnp.where(own_seen, matmul_nt(q[:, cols], k[:, cols]), 0.0).astype(BF16)
        mixed[:, cols] = matmul(intra, v[:, cols])
    loads[4].wait()
    loads[5].wait()
    for i, cols in enumerate(head_cols):
        gates[:, cols] = jax.nn.sigmoid(g[:, cols].astype(F32)) * gain[i : i + 1].astype(F32)

    pl.when(((c == 0) & (z >= 2)) | ((c == 1) & (z + 2 < groups)))(lambda: pl.semaphore_wait(hop_sem, 1))
    send_far(state, states, state_send, state_recv, c == 1)
    signal_if((c == 0) & (z >= 2), later_sem, (z - 2, 1, h))
    gather(states, state_send, state_recv)
    gathered(states, state_recv)
    loads[6].wait()
    spread(sk, keys, key_send, key_recv)
    doc_rows = [states[j, columns : columns + 1, :].astype(F32) for j in range(REACH)]
    for cols in head_cols:
        q_f32 = q[:, cols].astype(F32)
        carried = None
        for j in range(REACH):
            last = doc_rows[j][:, tokens - 1 :]
            part = matmul(jnp.where(doc_col == last, q_f32, 0.0).astype(BF16), states[j, cols, :])
            carried = part if carried is None else carried + part
        mixed[:, cols] += carried

    square = mixed[...] * mixed[...]
    own_row[...] = matmul_nt(jnp.ones((8, heads * DH), BF16), square.astype(BF16))[:1]

    pl.when(block > 0)(lambda: pl.semaphore_wait(ring_sem, 2))
    pl.when(first)(lambda: pl.semaphore_wait(barrier, len(near_heads) + len(far_heads)))
    for d in range(1, y_chips):
        remote(own_row, rows_y.at[y], y_send, y_recv, (z, c, column_head(d))).start()
    rows_y[y] = own_row[...]
    mid[...] = (mixed[...] * gates[...]).astype(BF16)
    spread(mid, mids, mid_send, mid_recv)
    gather(keys, key_send, key_recv, c == 0)

    y_span = rows_y.at[pl.ds(0, y_chips - 1)]
    pltpu.make_async_copy(y_span, y_span, y_recv).wait()
    column_row = rows_x.at[0, x]
    column_row[...] = jnp.sum(rows_y[...], axis=0)
    after = jnp.minimum(REACH, blocks - 1 - block)
    pl.when(after > 0)(lambda: pl.semaphore_wait(later_sem, after))
    for j in range(REACH + 1):

        @pl.when(block + j < blocks)
        def _(j=j):
            for d in range(0 if j else 1, x_chips):
                device = (*place(block + j), row_head(d))
                remote(column_row, rows_x.at[j, x], x_send.at[j], x_recv.at[j], device).start()

    gather(keys, key_send, key_recv, c == 1)
    gather(mids, mid_send, mid_recv)

    loads[7].wait()
    gathered(keys, key_recv)
    scale = 1.0 / math.sqrt(DH)
    for i, cols in enumerate(head_cols):
        query = sq[:, cols]
        parts = [jnp.where(own_seen, matmul_nt(query, sk[:, cols]) * scale, -jnp.inf)]
        for j in range(REACH):
            seen = doc_col == doc_rows[j]
            parts.append(jnp.where(seen, matmul_nt(query, keys[j, :, cols]) * scale, -jnp.inf))
        top = jnp.maximum(jnp.maximum(parts[0], parts[1]), jnp.maximum(parts[2], parts[3]))
        top = jnp.max(top, axis=1, keepdims=True)
        parts = [jnp.exp(part - top) for part in parts]
        total = jnp.sum(parts[0] + parts[1] + parts[2] + parts[3], axis=1, keepdims=True)
        for j, part in enumerate(parts):
            weights[i, j] = part / total

    def x_span(j):
        return rows_x.at[j, pl.ds(0, x_chips if j else x_chips - 1)]

    def inverse_norm(j):
        pl.when(block >= j)(pltpu.make_async_copy(x_span(j), x_span(j), x_recv.at[j]).wait)
        return lax.rsqrt(jnp.sum(rows_x[j], axis=0) / total_columns + 1e-05)

    inverse = inverse_norm(0)
    inverse_col = column(inverse)
    for cols in head_cols:
        out[0, :, cols] = (mixed[:, cols] * gates[:, cols] * inverse_col).astype(BF16)

    def attend(j, values):
        norm = inverse if j == 0 else inverse_norm(j)
        return [matmul((weights[i, j] * norm).astype(BF16), values[:, cols]) for i, cols in enumerate(head_cols)]

    results = attend(0, mid)
    gathered(mids, mid_recv)
    for j in range(REACH, 0, -1):
        results = [result + part for result, part in zip(results, attend(j, mids.at[j - 1]))]
    for result, cols in zip(results, head_cols):
        out[1, :, cols] = result.astype(BF16)

    for condition, copy in waits:
        pl.when(condition)(copy.wait_send)
    pltpu.make_async_copy(y_span, y_span, y_send).wait()
    for j in range(REACH + 1):
        pl.when(block + j < blocks)(pltpu.make_async_copy(x_span(j), x_span(j), x_send.at[j]).wait)


def per_device(mesh, *args):
    q, k, v, g, gain, seg, sq, sk = args
    tokens, columns = q.shape
    groups = mesh.shape["outer"]
    x_chips = min(X_CHIPS, mesh.shape["heads"])
    y_chips = mesh.shape["heads"] // x_chips
    total_columns = columns * mesh.shape["heads"]
    seg = seg.reshape(1, tokens)
    gain = gain.reshape(columns // DH, DH)
    dma = pltpu.SemaphoreType.DMA
    regular = pltpu.SemaphoreType.REGULAR
    block = (tokens, columns)
    stacked = (columns + 16, DH)
    outs = pl.pallas_call(
        functools.partial(kernel, groups, x_chips, y_chips, total_columns),
        out_shape=pltpu.VMEM((2,) + block, BF16),
        in_specs=[pl.BlockSpec(memory_space=pl.ANY)] * 8,
        out_specs=pl.BlockSpec(memory_space=pltpu.VMEM),
        scratch_shapes=[
            pltpu.VMEM(block, BF16), pltpu.VMEM(block, BF16), pltpu.VMEM(block, BF16), pltpu.VMEM(block, BF16),
            pltpu.VMEM((columns // DH, DH), BF16), pltpu.VMEM((1, tokens), jnp.int32),
            pltpu.VMEM(block, BF16), pltpu.VMEM(block, BF16),
            pltpu.VMEM(stacked, BF16), pltpu.VMEM((REACH,) + stacked, BF16),
            pltpu.VMEM((REACH,) + block, BF16),
            pltpu.VMEM(block, BF16), pltpu.VMEM((REACH,) + block, BF16),
            pltpu.VMEM((1, tokens), F32),
            pltpu.VMEM((y_chips, 1, tokens), F32),
            pltpu.VMEM((REACH + 1, x_chips, 1, tokens), F32),
            pltpu.VMEM(block, F32), pltpu.VMEM(block, F32),
            pltpu.VMEM((columns // DH, REACH + 1, tokens, tokens), F32),
            dma((8,)),
            dma((3,)), dma((REACH,)), dma((3,)), dma((REACH,)), dma((3,)), dma((REACH,)),
            dma, dma, dma((REACH + 1,)), dma((REACH + 1,)),
            regular, regular, regular, regular,
        ],
        compiler_params=pltpu.CompilerParams(collective_id=0, has_side_effects=True),
    )(q, k, v, g, gain, seg, sq, sk)
    return outs[0], outs[1]


def solution(mesh):
    block = P(("outer", "inner"), "heads")
    return jax.shard_map(
        functools.partial(per_device, mesh),
        mesh=mesh,
        in_specs=(block, block, block, block, P("heads"), P(("outer", "inner")), block, block),
        out_specs=(block, block),
        check_vma=False,
    )
```

```python
import functools
import math

import jax
import jax.numpy as jnp
from jax import lax
from jax.experimental import pallas as pl
from jax.experimental.pallas import tpu as pltpu
from jax.sharding import PartitionSpec as P

DH = 128
X_CHIPS = 4
REACH = 3
MESH = pl.DeviceIdType.MESH
F32 = jnp.float32
BF16 = jnp.bfloat16


def matmul(a, b):
    return jnp.dot(a, b, preferred_element_type=F32)


def matmul_nt(a, b):
    return lax.dot_general(a, b, (((1,), (1,)), ((), ())), preferred_element_type=F32)


def matmul_tn(a, b):
    return lax.dot_general(a, b, (((0,), (0,)), ((), ())), preferred_element_type=F32)


def column(row):
    n = row.shape[1]
    return jnp.transpose(jnp.broadcast_to(row, (n, n)))


def kernel(
    groups, x_chips, y_chips, total_columns,
    q_in, k_in, v_in, g_in, gain_in, seg_in, sq_in, sk_in,
    out,
    q, k, v, g, gain, seg, sq, sk,
    state, states, keys, mid, mids, own_row, rows_y, rows_x,
    gates, mixed, weights,
    load_sem, state_send, state_recv, key_send, key_recv, mid_send, mid_recv,
    y_send, y_recv, x_send, x_recv, hop_sem, ring_sem, later_sem, go_sem,
):
    z = lax.axis_index("outer")
    c = lax.axis_index("inner")
    h = lax.axis_index("heads")
    y, x = h // x_chips, h % x_chips
    block = 2 * z + c
    blocks = 2 * groups
    tokens = q.shape[0]
    heads = q.shape[1] // DH
    head_cols = [slice(i * DH, (i + 1) * DH) for i in range(heads)]

    def place(n):
        return n // 2, n % 2

    def row_head(d):
        return y * x_chips + lax.rem(x + d, x_chips)

    def column_head(d):
        return lax.rem(y + d, y_chips) * x_chips + x

    other = (z, 1 - c, h)
    has_relay = z >= 1
    barrier = pltpu.get_barrier_semaphore()

    def signal(sem, device):
        pl.semaphore_signal(sem, inc=1, device_id=device, device_id_type=MESH)

    def signal_if(condition, sem, device):
        pl.when(condition)(lambda: signal(sem, device))

    loads = [
        pltpu.make_async_copy(a, b, load_sem.at[i])
        for i, (a, b) in enumerate(
            ((seg_in, seg), (k_in, k), (v_in, v), (q_in, q), (gain_in, gain), (g_in, g), (sk_in, sk), (sq_in, sq))
        )
    ]
    for copy in loads[:3]:
        copy.start()

    first = block == 0
    earlier = [(True, block - 1), (True, block - 2), (c == 1, block - 3)]
    later = [(True, block + 1), (True, block + 2), (c == 0, block + 3)]
    reached = [(near & (n >= 1), n) for near, n in earlier] + [(near & (n < blocks), n) for near, n in later]
    heard = [near & (n >= 0) for near, n in earlier] + [near & (n < blocks) & (block > 0) for near, n in later]
    near_heads = [row_head(d) for d in range(1, x_chips)] + [column_head(d) for d in (1, y_chips - 1, 2, y_chips - 2)]
    for condition, n in reached:
        signal_if(condition, barrier, (*place(n), h))
    for head in near_heads:
        signal(barrier, (z, c, head))
    far_heads = [column_head(d) for d in range(3, y_chips - 2)]
    for head in far_heads:
        signal_if(first, barrier, (z, c, head))
    for copy in loads[3:]:
        copy.start()

    columns = heads * DH
    for j in range(1, REACH + 1):

        @pl.when(block < j)
        def _(j=j):
            states[j - 1, :columns] = jnp.zeros((columns, DH), BF16)
            states[j - 1, columns:] = jnp.full((states.shape[1] - columns, DH), -1.0, BF16)
            keys[j - 1] = jnp.zeros(keys.shape[1:], BF16)
            mids[j - 1] = jnp.zeros(mids.shape[1:], BF16)
            rows_x[j] = jnp.zeros(rows_x.shape[1:], F32)

    for copy in loads[:3]:
        copy.wait()
    doc_row = seg[...].astype(F32)
    doc_col = column(doc_row)
    kept = doc_col == doc_row[:, tokens - 1 :]
    for cols in head_cols:
        masked = jnp.where(kept, k[:, cols].astype(F32), 0.0).astype(BF16)
        state[cols, :] = matmul_tn(masked, v[:, cols]).astype(BF16)

    state[columns:, :] = jnp.broadcast_to(doc_row, (state.shape[0] - columns, tokens)).astype(BF16)

    def count(*conditions):
        return sum(condition.astype(jnp.int32) for condition in conditions)

    pl.when(block > 0)(lambda: pl.semaphore_wait(barrier, len(near_heads) + count(*heard)))
    pl.when(first)(lambda: pl.semaphore_wait(go_sem, 1))
    signal_if(block == 1, go_sem, other)

    middle = (c == 0) & (z >= 1) & (z + 1 < groups)
    signal_if(middle, hop_sem, (z - 1, 1, h))
    signal_if(middle, hop_sem, (z + 1, 0, h))

    waits = []

    def remote(src, dst, send_sem, recv_sem, device):
        return pltpu.make_async_remote_copy(
            src_ref=src, dst_ref=dst, send_sem=send_sem, recv_sem=recv_sem, device_id=device, device_id_type=MESH
        )

    def send(condition, *args):
        copy = remote(*args)
        pl.when(condition)(copy.start)
        waits.append((condition, copy))

    def arrived(condition, dst, slot, recvs):
        pl.when(condition)(pltpu.make_async_copy(dst.at[slot], dst.at[slot], recvs.at[slot]).wait)

    relay_slot, rest_slot = 2 * c, 2 - 2 * c
    has_rest = z + 2 * c >= 2

    def send_near(src, dst, sends, recvs):
        send(z + c < groups, src, dst.at[0], sends.at[0], recvs.at[0], (z + c, 1 - c, h))

    def send_far(src, dst, sends, recvs, condition=True):
        there = condition & (z + 1 + c < groups)
        send(there, src, dst.at[2], sends.at[1], recvs.at[2], (z + 1 + c, 1 - c, h))

    def spread(src, dst, sends, recvs):
        send_near(src, dst, sends, recvs)
        send_far(src, dst, sends, recvs)

    def gather(dst, sends, recvs, condition=True):
        here = has_relay & condition
        arrived(here, dst, relay_slot, recvs)
        send(here, dst.at[relay_slot], dst.at[1], sends.at[2], recvs.at[1], other)

    def gathered(dst, recvs):
        arrived(has_rest, dst, rest_slot, recvs)
        arrived(has_relay, dst, 1, recvs)

    send_near(state, states, state_send, state_recv)
    send_far(state, states, state_send, state_recv, c == 0)
    for d in (2, y_chips - 2):
        signal_if(block > 0, ring_sem, (z, c, column_head(d)))
    for j in range(1, REACH + 1):
        signal_if((block >= j) & ((c == 1) if j == REACH else True), later_sem, (*place(block - j), h))

    loads[3].wait()
    at_t = lax.broadcasted_iota(jnp.int32, (tokens, tokens), 0)
    at_s = lax.broadcasted_iota(jnp.int32, (tokens, tokens), 1)
    own_seen = (at_t >= at_s) & (doc_col == doc_row)
    for cols in head_cols:
        intra = jnp.where(own_seen, matmul_nt(q[:, cols], k[:, cols]), 0.0).astype(BF16)
        mixed[:, cols] = matmul(intra, v[:, cols])
    loads[4].wait()
    loads[5].wait()
    for i, cols in enumerate(head_cols):
        gates[:, cols] = jax.nn.sigmoid(g[:, cols].astype(F32)) * gain[i : i + 1].astype(F32)

    pl.when(((c == 0) & (z >= 2)) | ((c == 1) & (z + 2 < groups)))(lambda: pl.semaphore_wait(hop_sem, 1))
    send_far(state, states, state_send, state_recv, c == 1)
    signal_if((c == 0) & (z >= 2), later_sem, (z - 2, 1, h))
    gather(states, state_send, state_recv)
    gathered(states, state_recv)
    loads[6].wait()
    spread(sk, keys, key_send, key_recv)
    doc_rows = [states[j, columns : columns + 1, :].astype(F32) for j in range(REACH)]
    for cols in head_cols:
        carried = None
        for j in range(REACH):
            last = doc_rows[j][:, tokens - 1 :]
            part = jnp.where(doc_col == last, matmul(q[:, cols], states[j, cols, :]), 0.0)
            carried = part if carried is None else carried + part
        mixed[:, cols] += carried

    square = mixed[...] * mixed[...]
    own_row[...] = matmul_nt(jnp.ones((8, heads * DH), BF16), square.astype(BF16))[:1]

    pl.when(block > 0)(lambda: pl.semaphore_wait(ring_sem, 2))
    pl.when(first)(lambda: pl.semaphore_wait(barrier, len(near_heads) + len(far_heads)))
    for d in sorted(range(1, y_chips), key=lambda d: abs(d - y_chips // 2)):
        remote(own_row, rows_y.at[y], y_send, y_recv, (z, c, column_head(d))).start()
    rows_y[y] = own_row[...]
    mid[...] = (mixed[...] * gates[...]).astype(BF16)
    spread(mid, mids, mid_send, mid_recv)
    gather(keys, key_send, key_recv, c == 0)

    y_span = rows_y.at[pl.ds(0, y_chips - 1)]
    pltpu.make_async_copy(y_span, y_span, y_recv).wait()
    column_row = rows_x.at[0, x]
    column_row[...] = jnp.sum(rows_y[...], axis=0)
    after = jnp.minimum(REACH, blocks - 1 - block)
    pl.when(after > 0)(lambda: pl.semaphore_wait(later_sem, after))
    for j in range(REACH + 1):

        @pl.when(block + j < blocks)
        def _(j=j):
            for d in (2, 1, 3) + ((0,) if j else ()):
                device = (*place(block + j), row_head(d))
                remote(column_row, rows_x.at[j, x], x_send.at[j], x_recv.at[j], device).start()

    gather(keys, key_send, key_recv, c == 1)
    gather(mids, mid_send, mid_recv)

    loads[7].wait()
    gathered(keys, key_recv)
    scale = 1.0 / math.sqrt(DH)
    for i, cols in enumerate(head_cols):
        query = sq[:, cols]
        parts = [jnp.where(own_seen, matmul_nt(query, sk[:, cols]) * scale, -jnp.inf)]
        for j in range(REACH):
            seen = doc_col == doc_rows[j]
            parts.append(jnp.where(seen, matmul_nt(query, keys[j, :, cols]) * scale, -jnp.inf))
        top = jnp.maximum(jnp.maximum(parts[0], parts[1]), jnp.maximum(parts[2], parts[3]))
        top = jnp.max(top, axis=1, keepdims=True)
        parts = [jnp.exp(part - top) for part in parts]
        total = jnp.sum(parts[0] + parts[1] + parts[2] + parts[3], axis=1, keepdims=True)
        for j, part in enumerate(parts):
            weights[i, j] = part / total

    def x_span(j):
        return rows_x.at[j, pl.ds(0, x_chips if j else x_chips - 1)]

    def attend(j, norm, values):
        return [matmul((weights[i, j] * norm).astype(BF16), values[:, cols]) for i, cols in enumerate(head_cols)]

    def both(left, right):
        return [one + other_one for one, other_one in zip(left, right)]

    gathered(mids, mid_recv)
    for j in range(REACH + 1):
        pl.when(block >= j)(pltpu.make_async_copy(x_span(j), x_span(j), x_recv.at[j]).wait)
    norms = [lax.rsqrt(jnp.sum(rows_x[j], axis=0) / total_columns + 1e-05) for j in range(REACH + 1)]
    inverse = norms[0]
    results = attend(0, inverse, mid)
    for j in range(1, REACH + 1):
        results = both(results, attend(j, norms[j], mids.at[j - 1]))
    inverse_col = column(inverse)
    for cols in head_cols:
        out[0, :, cols] = (mixed[:, cols] * gates[:, cols] * inverse_col).astype(BF16)
    for result, cols in zip(results, head_cols):
        out[1, :, cols] = result.astype(BF16)

    for condition, copy in waits:
        pl.when(condition)(copy.wait_send)
    pltpu.make_async_copy(y_span, y_span, y_send).wait()
    for j in range(REACH + 1):
        pl.when(block + j < blocks)(pltpu.make_async_copy(x_span(j), x_span(j), x_send.at[j]).wait)


def per_device(mesh, *args):
    q, k, v, g, gain, seg, sq, sk = args
    tokens, columns = q.shape
    groups = mesh.shape["outer"]
    x_chips = min(X_CHIPS, mesh.shape["heads"])
    y_chips = mesh.shape["heads"] // x_chips
    total_columns = columns * mesh.shape["heads"]
    seg = seg.reshape(1, tokens)
    gain = gain.reshape(columns // DH, DH)
    dma = pltpu.SemaphoreType.DMA
    regular = pltpu.SemaphoreType.REGULAR
    block = (tokens, columns)
    stacked = (columns + 16, DH)
    outs = pl.pallas_call(
        functools.partial(kernel, groups, x_chips, y_chips, total_columns),
        out_shape=pltpu.VMEM((2,) + block, BF16),
        in_specs=[pl.BlockSpec(memory_space=pl.ANY)] * 8,
        out_specs=pl.BlockSpec(memory_space=pltpu.VMEM),
        scratch_shapes=[
            pltpu.VMEM(block, BF16), pltpu.VMEM(block, BF16), pltpu.VMEM(block, BF16), pltpu.VMEM(block, BF16),
            pltpu.VMEM((columns // DH, DH), BF16), pltpu.VMEM((1, tokens), jnp.int32),
            pltpu.VMEM(block, BF16), pltpu.VMEM(block, BF16),
            pltpu.VMEM(stacked, BF16), pltpu.VMEM((REACH,) + stacked, BF16),
            pltpu.VMEM((REACH,) + block, BF16),
            pltpu.VMEM(block, BF16), pltpu.VMEM((REACH,) + block, BF16),
            pltpu.VMEM((1, tokens), F32),
            pltpu.VMEM((y_chips, 1, tokens), F32),
            pltpu.VMEM((REACH + 1, x_chips, 1, tokens), F32),
            pltpu.VMEM(block, F32), pltpu.VMEM(block, F32),
            pltpu.VMEM((columns // DH, REACH + 1, tokens, tokens), F32),
            dma((8,)),
            dma((3,)), dma((REACH,)), dma((3,)), dma((REACH,)), dma((3,)), dma((REACH,)),
            dma, dma, dma((REACH + 1,)), dma((REACH + 1,)),
            regular, regular, regular, regular,
        ],
        compiler_params=pltpu.CompilerParams(collective_id=0, has_side_effects=True),
    )(q, k, v, g, gain, seg, sq, sk)
    return outs[0], outs[1]


def solution(mesh):
    block = P(("outer", "inner"), "heads")
    return jax.shard_map(
        functools.partial(per_device, mesh),
        mesh=mesh,
        in_specs=(block, block, block, block, P("heads"), P(("outer", "inner")), block, block),
        out_specs=(block, block),
        check_vma=False,
    )
```

```python
import functools
import math

import jax
import jax.numpy as jnp
from jax import lax
from jax.experimental import pallas as pl
from jax.experimental.pallas import tpu as pltpu
from jax.sharding import PartitionSpec as P

DH = 128
X_CHIPS = 4
REACH = 3
MESH = pl.DeviceIdType.MESH
F32 = jnp.float32
BF16 = jnp.bfloat16


def matmul(a, b):
    return jnp.dot(a, b, preferred_element_type=F32)


def matmul_nt(a, b):
    return lax.dot_general(a, b, (((1,), (1,)), ((), ())), preferred_element_type=F32)


def matmul_tn(a, b):
    return lax.dot_general(a, b, (((0,), (0,)), ((), ())), preferred_element_type=F32)


def column(row):
    n = row.shape[1]
    return jnp.transpose(jnp.broadcast_to(row, (n, n)))


def kernel(
    groups, x_chips, y_chips, total_columns,
    q_in, k_in, v_in, g_in, gain_in, seg_in, sq_in, sk_in,
    out,
    q, k, v, g, gain, seg, sq, sk,
    state, states, keys, mid, mids, own_row, rows_y, rows_x,
    gates, mixed, weights,
    load_sem, state_send, state_recv, key_send, key_recv, mid_send, mid_recv,
    y_send, y_recv, x_send, x_recv, hop_sem, ring_sem, later_sem, go_sem, near_sem,
):
    z = lax.axis_index("outer")
    c = lax.axis_index("inner")
    h = lax.axis_index("heads")
    y, x = h // x_chips, h % x_chips
    block = 2 * z + c
    blocks = 2 * groups
    tokens = q.shape[0]
    heads = q.shape[1] // DH
    head_cols = [slice(i * DH, (i + 1) * DH) for i in range(heads)]

    def place(n):
        return n // 2, n % 2

    def row_head(d):
        return y * x_chips + lax.rem(x + d, x_chips)

    def column_head(d):
        return lax.rem(y + d, y_chips) * x_chips + x

    other = (z, 1 - c, h)
    has_relay = z >= 1
    barrier = pltpu.get_barrier_semaphore()

    def signal(sem, device):
        pl.semaphore_signal(sem, inc=1, device_id=device, device_id_type=MESH)

    def signal_if(condition, sem, device):
        pl.when(condition)(lambda: signal(sem, device))

    loads = [
        pltpu.make_async_copy(a, b, load_sem.at[i])
        for i, (a, b) in enumerate(
            ((seg_in, seg), (k_in, k), (v_in, v), (q_in, q), (gain_in, gain), (g_in, g), (sk_in, sk), (sq_in, sq))
        )
    ]
    for copy in loads[:3]:
        copy.start()

    first = block == 0
    earlier = [(True, block - 1), (True, block - 2), (c == 1, block - 3)]
    later = [(True, block + 1), (True, block + 2), (c == 0, block + 3)]
    reached = [(near & (n >= 1), n) for near, n in earlier] + [(near & (n < blocks), n) for near, n in later]
    heard = [near & (n >= 0) for near, n in earlier] + [near & (n < blocks) & (block > 0) for near, n in later]
    near_heads = [row_head(1), row_head(x_chips - 1), column_head(1), column_head(y_chips - 1)]
    for condition, n in reached:
        signal_if(condition, barrier, (*place(n), h))
    for head in near_heads:
        signal(barrier, (z, c, head))
    far_heads = [row_head(d) for d in range(2, x_chips - 1)] + [column_head(d) for d in range(2, y_chips - 1)]
    for head in far_heads:
        signal_if(first, barrier, (z, c, head))
    for copy in loads[3:]:
        copy.start()

    columns = heads * DH
    for j in range(1, REACH + 1):

        @pl.when(block < j)
        def _(j=j):
            states[j - 1, :columns] = jnp.zeros((columns, DH), BF16)
            states[j - 1, columns:] = jnp.full((states.shape[1] - columns, DH), -1.0, BF16)
            keys[j - 1] = jnp.zeros(keys.shape[1:], BF16)
            mids[j - 1] = jnp.zeros(mids.shape[1:], BF16)
            rows_x[j] = jnp.zeros(rows_x.shape[1:], F32)

    for copy in loads[:3]:
        copy.wait()
    doc_row = seg[...].astype(F32)
    doc_col = column(doc_row)
    kept = doc_col == doc_row[:, tokens - 1 :]
    for cols in head_cols:
        masked = jnp.where(kept, k[:, cols].astype(F32), 0.0).astype(BF16)
        state[cols, :] = matmul_tn(masked, v[:, cols]).astype(BF16)

    state[columns:, :] = jnp.broadcast_to(doc_row, (state.shape[0] - columns, tokens)).astype(BF16)

    def count(*conditions):
        return sum(condition.astype(jnp.int32) for condition in conditions)

    pl.when(block > 0)(lambda: pl.semaphore_wait(barrier, len(near_heads) + count(*heard)))
    pl.when(first)(lambda: pl.semaphore_wait(go_sem, 1))
    signal_if(block == 1, go_sem, other)

    middle = (c == 0) & (z >= 1) & (z + 1 < groups)
    signal_if(middle, hop_sem, (z - 1, 1, h))
    signal_if(middle, hop_sem, (z + 1, 0, h))

    waits = []

    def remote(src, dst, send_sem, recv_sem, device):
        return pltpu.make_async_remote_copy(
            src_ref=src, dst_ref=dst, send_sem=send_sem, recv_sem=recv_sem, device_id=device, device_id_type=MESH
        )

    def send(condition, *args):
        copy = remote(*args)
        pl.when(condition)(copy.start)
        waits.append((condition, copy))

    def arrived(condition, dst, slot, recvs):
        pl.when(condition)(pltpu.make_async_copy(dst.at[slot], dst.at[slot], recvs.at[slot]).wait)

    relay_slot, rest_slot = 2 * c, 2 - 2 * c
    has_rest = z + 2 * c >= 2

    def send_near(src, dst, sends, recvs):
        send(z + c < groups, src, dst.at[0], sends.at[0], recvs.at[0], (z + c, 1 - c, h))

    def send_far(src, dst, sends, recvs, condition=True):
        there = condition & (z + 1 + c < groups)
        send(there, src, dst.at[2], sends.at[1], recvs.at[2], (z + 1 + c, 1 - c, h))

    def spread(src, dst, sends, recvs):
        send_near(src, dst, sends, recvs)
        send_far(src, dst, sends, recvs)

    def gather(dst, sends, recvs, condition=True):
        here = has_relay & condition
        arrived(here, dst, relay_slot, recvs)
        send(here, dst.at[relay_slot], dst.at[1], sends.at[2], recvs.at[1], other)

    def gathered(dst, recvs):
        arrived(has_rest, dst, rest_slot, recvs)
        arrived(has_relay, dst, 1, recvs)

    send_near(state, states, state_send, state_recv)
    send_far(state, states, state_send, state_recv, c == 0)
    for head in near_heads:
        signal_if(block > 0, near_sem, (z, c, head))

    loads[3].wait()
    at_t = lax.broadcasted_iota(jnp.int32, (tokens, tokens), 0)
    at_s = lax.broadcasted_iota(jnp.int32, (tokens, tokens), 1)
    own_seen = (at_t >= at_s) & (doc_col == doc_row)
    for cols in head_cols:
        intra = jnp.where(own_seen, matmul_nt(q[:, cols], k[:, cols]), 0.0).astype(BF16)
        mixed[:, cols] = matmul(intra, v[:, cols])
    loads[4].wait()
    loads[5].wait()
    for i, cols in enumerate(head_cols):
        gates[:, cols] = jax.nn.sigmoid(g[:, cols].astype(F32)) * gain[i : i + 1].astype(F32)

    pl.when(block > 0)(lambda: pl.semaphore_wait(near_sem, len(near_heads)))
    for d in (2, y_chips - 2):
        signal_if(block > 0, ring_sem, (z, c, column_head(d)))
    for j in range(1, REACH + 1):
        signal_if((block >= j) & ((c == 1) if j == REACH else True), later_sem, (*place(block - j), h))

    pl.when((c == 1) & (z + 2 < groups))(lambda: pl.semaphore_wait(hop_sem, 1))
    send_far(state, states, state_send, state_recv, c == 1)
    gather(states, state_send, state_recv)
    pl.when((c == 0) & (z >= 2))(lambda: pl.semaphore_wait(hop_sem, 1))
    signal_if((c == 0) & (z >= 2), later_sem, (z - 2, 1, h))
    gathered(states, state_recv)
    loads[6].wait()
    spread(sk, keys, key_send, key_recv)
    doc_rows = [states[j, columns : columns + 1, :].astype(F32) for j in range(REACH)]
    for cols in head_cols:
        carried = None
        for j in range(REACH):
            last = doc_rows[j][:, tokens - 1 :]
            part = jnp.where(doc_col == last, matmul(q[:, cols], states[j, cols, :]), 0.0)
            carried = part if carried is None else carried + part
        mixed[:, cols] += carried

    square = mixed[...] * mixed[...]
    own_row[...] = matmul_nt(jnp.ones((8, heads * DH), BF16), square.astype(BF16))[:1]

    pl.when(block > 0)(lambda: pl.semaphore_wait(ring_sem, 2))
    pl.when(first)(lambda: pl.semaphore_wait(barrier, len(near_heads) + len(far_heads)))
    for d in sorted(range(1, y_chips), key=lambda d: abs(d - y_chips // 2)):
        remote(own_row, rows_y.at[y], y_send, y_recv, (z, c, column_head(d))).start()
    rows_y[y] = own_row[...]
    mid[...] = (mixed[...] * gates[...]).astype(BF16)
    spread(mid, mids, mid_send, mid_recv)
    gather(keys, key_send, key_recv, c == 0)

    y_span = rows_y.at[pl.ds(0, y_chips - 1)]
    pltpu.make_async_copy(y_span, y_span, y_recv).wait()
    column_row = rows_x.at[0, x]
    column_row[...] = jnp.sum(rows_y[...], axis=0)
    after = jnp.minimum(REACH, blocks - 1 - block)
    pl.when(after > 0)(lambda: pl.semaphore_wait(later_sem, after))
    for j in range(REACH + 1):

        @pl.when(block + j < blocks)
        def _(j=j):
            for d in (2, 1, 3) + ((0,) if j else ()):
                device = (*place(block + j), row_head(d))
                remote(column_row, rows_x.at[j, x], x_send.at[j], x_recv.at[j], device).start()

    gather(keys, key_send, key_recv, c == 1)
    gather(mids, mid_send, mid_recv)

    loads[7].wait()
    gathered(keys, key_recv)
    scale = 1.0 / math.sqrt(DH)
    for i, cols in enumerate(head_cols):
        query = sq[:, cols]
        parts = [jnp.where(own_seen, matmul_nt(query, sk[:, cols]) * scale, -jnp.inf)]
        for j in range(REACH):
            seen = doc_col == doc_rows[j]
            parts.append(jnp.where(seen, matmul_nt(query, keys[j, :, cols]) * scale, -jnp.inf))
        top = jnp.maximum(jnp.maximum(parts[0], parts[1]), jnp.maximum(parts[2], parts[3]))
        top = jnp.max(top, axis=1, keepdims=True)
        parts = [jnp.exp(part - top) for part in parts]
        total = jnp.sum(parts[0] + parts[1] + parts[2] + parts[3], axis=1, keepdims=True)
        for j, part in enumerate(parts):
            weights[i, j] = part / total

    def x_span(j):
        return rows_x.at[j, pl.ds(0, x_chips if j else x_chips - 1)]

    def attend(j, norm, values):
        return [matmul((weights[i, j] * norm).astype(BF16), values[:, cols]) for i, cols in enumerate(head_cols)]

    def both(left, right):
        return [one + other_one for one, other_one in zip(left, right)]

    gathered(mids, mid_recv)
    for j in range(REACH + 1):
        pl.when(block >= j)(pltpu.make_async_copy(x_span(j), x_span(j), x_recv.at[j]).wait)
    norms = [lax.rsqrt(jnp.sum(rows_x[j], axis=0) / total_columns + 1e-05) for j in range(REACH + 1)]
    inverse = norms[0]
    results = attend(0, inverse, mid)
    for j in range(1, REACH + 1):
        results = both(results, attend(j, norms[j], mids.at[j - 1]))
    inverse_col = column(inverse)
    for cols in head_cols:
        out[0, :, cols] = (mixed[:, cols] * gates[:, cols] * inverse_col).astype(BF16)
    for result, cols in zip(results, head_cols):
        out[1, :, cols] = result.astype(BF16)

    for condition, copy in waits:
        pl.when(condition)(copy.wait_send)
    pltpu.make_async_copy(y_span, y_span, y_send).wait()
    for j in range(REACH + 1):
        pl.when(block + j < blocks)(pltpu.make_async_copy(x_span(j), x_span(j), x_send.at[j]).wait)


def per_device(mesh, *args):
    q, k, v, g, gain, seg, sq, sk = args
    tokens, columns = q.shape
    groups = mesh.shape["outer"]
    x_chips = min(X_CHIPS, mesh.shape["heads"])
    y_chips = mesh.shape["heads"] // x_chips
    total_columns = columns * mesh.shape["heads"]
    seg = seg.reshape(1, tokens)
    gain = gain.reshape(columns // DH, DH)
    dma = pltpu.SemaphoreType.DMA
    regular = pltpu.SemaphoreType.REGULAR
    block = (tokens, columns)
    stacked = (columns + 16, DH)
    outs = pl.pallas_call(
        functools.partial(kernel, groups, x_chips, y_chips, total_columns),
        out_shape=pltpu.VMEM((2,) + block, BF16),
        in_specs=[pl.BlockSpec(memory_space=pl.ANY)] * 8,
        out_specs=pl.BlockSpec(memory_space=pltpu.VMEM),
        scratch_shapes=[
            pltpu.VMEM(block, BF16), pltpu.VMEM(block, BF16), pltpu.VMEM(block, BF16), pltpu.VMEM(block, BF16),
            pltpu.VMEM((columns // DH, DH), BF16), pltpu.VMEM((1, tokens), jnp.int32),
            pltpu.VMEM(block, BF16), pltpu.VMEM(block, BF16),
            pltpu.VMEM(stacked, BF16), pltpu.VMEM((REACH,) + stacked, BF16),
            pltpu.VMEM((REACH,) + block, BF16),
            pltpu.VMEM(block, BF16), pltpu.VMEM((REACH,) + block, BF16),
            pltpu.VMEM((1, tokens), F32),
            pltpu.VMEM((y_chips, 1, tokens), F32),
            pltpu.VMEM((REACH + 1, x_chips, 1, tokens), F32),
            pltpu.VMEM(block, F32), pltpu.VMEM(block, F32),
            pltpu.VMEM((columns // DH, REACH + 1, tokens, tokens), F32),
            dma((8,)),
            dma((3,)), dma((REACH,)), dma((3,)), dma((REACH,)), dma((3,)), dma((REACH,)),
            dma, dma, dma((REACH + 1,)), dma((REACH + 1,)),
            regular, regular, regular, regular, regular,
        ],
        compiler_params=pltpu.CompilerParams(collective_id=0, has_side_effects=True),
    )(q, k, v, g, gain, seg, sq, sk)
    return outs[0], outs[1]


def solution(mesh):
    block = P(("outer", "inner"), "heads")
    return jax.shard_map(
        functools.partial(per_device, mesh),
        mesh=mesh,
        in_specs=(block, block, block, block, P("heads"), P(("outer", "inner")), block, block),
        out_specs=(block, block),
        check_vma=False,
    )
```

```python
import functools
import math

import jax
import jax.numpy as jnp
from jax import lax
from jax.experimental import pallas as pl
from jax.experimental.pallas import tpu as pltpu
from jax.sharding import PartitionSpec as P

DH = 128
X_CHIPS = 4
REACH = 3
MESH = pl.DeviceIdType.MESH
F32 = jnp.float32
BF16 = jnp.bfloat16


def matmul(a, b):
    return jnp.dot(a, b, preferred_element_type=F32)


def matmul_nt(a, b):
    return lax.dot_general(a, b, (((1,), (1,)), ((), ())), preferred_element_type=F32)


def matmul_tn(a, b):
    return lax.dot_general(a, b, (((0,), (0,)), ((), ())), preferred_element_type=F32)


def column(row):
    n = row.shape[1]
    return jnp.transpose(jnp.broadcast_to(row, (n, n)))


def kernel(
    groups, x_chips, y_chips, total_columns,
    q_in, k_in, v_in, g_in, gain_in, seg_in, sq_in, sk_in,
    out,
    q, k, v, g, gain, seg, sq, sk,
    state, states, keys, mid, mids, own_row, rows_y, rows_x,
    gates, mixed, weights,
    load_sem, state_send, state_recv, key_send, key_recv, mid_send, mid_recv,
    y_send, y_recv, x_send, x_recv, hop_sem, ring_sem, later_sem, go_sem,
):
    z = lax.axis_index("outer")
    c = lax.axis_index("inner")
    h = lax.axis_index("heads")
    y, x = h // x_chips, h % x_chips
    block = 2 * z + c
    blocks = 2 * groups
    tokens = q.shape[0]
    heads = q.shape[1] // DH
    head_cols = [slice(i * DH, (i + 1) * DH) for i in range(heads)]

    def place(n):
        return n // 2, n % 2

    def row_head(d):
        return y * x_chips + lax.rem(x + d, x_chips)

    def column_head(d):
        return lax.rem(y + d, y_chips) * x_chips + x

    other = (z, 1 - c, h)
    has_relay = z >= 1
    barrier = pltpu.get_barrier_semaphore()

    def signal(sem, device):
        pl.semaphore_signal(sem, inc=1, device_id=device, device_id_type=MESH)

    def signal_if(condition, sem, device):
        pl.when(condition)(lambda: signal(sem, device))

    loads = [
        pltpu.make_async_copy(a, b, load_sem.at[i])
        for i, (a, b) in enumerate(
            ((seg_in, seg), (k_in, k), (v_in, v), (q_in, q), (gain_in, gain), (g_in, g), (sk_in, sk), (sq_in, sq))
        )
    ]
    for copy in loads[:3]:
        copy.start()

    first = block == 0
    earlier = [(True, block - 1), (True, block - 2), (c == 1, block - 3)]
    later = [(True, block + 1), (True, block + 2), (c == 0, block + 3)]
    reached = [(near & (n >= 1), n) for near, n in earlier] + [(near & (n < blocks), n) for near, n in later]
    heard = [near & (n >= 0) for near, n in earlier] + [near & (n < blocks) & (block > 0) for near, n in later]
    near_heads = [row_head(d) for d in range(1, x_chips)] + [column_head(d) for d in (1, y_chips - 1, 2, y_chips - 2)]
    for condition, n in reached:
        signal_if(condition, barrier, (*place(n), h))
    for head in near_heads:
        signal(barrier, (z, c, head))
    far_heads = [column_head(d) for d in range(3, y_chips - 2)]
    for head in far_heads:
        signal_if(first, barrier, (z, c, head))
    for copy in loads[3:]:
        copy.start()

    columns = heads * DH
    for j in range(1, REACH + 1):

        @pl.when(block < j)
        def _(j=j):
            states[j - 1, :columns] = jnp.zeros((columns, DH), BF16)
            states[j - 1, columns:] = jnp.full((states.shape[1] - columns, DH), -1.0, BF16)
            keys[j - 1] = jnp.zeros(keys.shape[1:], BF16)
            mids[j - 1] = jnp.zeros(mids.shape[1:], BF16)
            rows_x[j] = jnp.zeros(rows_x.shape[1:], F32)

    for copy in loads[:3]:
        copy.wait()
    doc_row = seg[...].astype(F32)
    doc_col = column(doc_row)
    kept = doc_col == doc_row[:, tokens - 1 :]
    for cols in head_cols:
        masked = jnp.where(kept, k[:, cols].astype(F32), 0.0).astype(BF16)
        state[cols, :] = matmul_tn(masked, v[:, cols]).astype(BF16)

    state[columns:, :] = jnp.broadcast_to(doc_row, (state.shape[0] - columns, tokens)).astype(BF16)

    def count(*conditions):
        return sum(condition.astype(jnp.int32) for condition in conditions)

    pl.when(block > 0)(lambda: pl.semaphore_wait(barrier, len(near_heads) + count(*heard)))
    pl.when(first)(lambda: pl.semaphore_wait(go_sem, 1))
    signal_if(block == 1, go_sem, other)

    middle = (c == 0) & (z >= 1) & (z + 1 < groups)
    signal_if(middle, hop_sem, (z - 1, 1, h))
    signal_if(middle, hop_sem, (z + 1, 0, h))

    waits = []

    def remote(src, dst, send_sem, recv_sem, device):
        return pltpu.make_async_remote_copy(
            src_ref=src, dst_ref=dst, send_sem=send_sem, recv_sem=recv_sem, device_id=device, device_id_type=MESH
        )

    def send(condition, *args):
        copy = remote(*args)
        pl.when(condition)(copy.start)
        waits.append((condition, copy))

    def arrived(condition, dst, slot, recvs):
        pl.when(condition)(pltpu.make_async_copy(dst.at[slot], dst.at[slot], recvs.at[slot]).wait)

    relay_slot, rest_slot = 2 * c, 2 - 2 * c
    has_rest = z + 2 * c >= 2

    def send_near(src, dst, sends, recvs):
        send(z + c < groups, src, dst.at[0], sends.at[0], recvs.at[0], (z + c, 1 - c, h))

    def send_far(src, dst, sends, recvs, condition=True):
        there = condition & (z + 1 + c < groups)
        send(there, src, dst.at[2], sends.at[1], recvs.at[2], (z + 1 + c, 1 - c, h))

    def spread(src, dst, sends, recvs):
        send_near(src, dst, sends, recvs)
        send_far(src, dst, sends, recvs)

    def gather(dst, sends, recvs, condition=True):
        here = has_relay & condition
        arrived(here, dst, relay_slot, recvs)
        send(here, dst.at[relay_slot], dst.at[1], sends.at[2], recvs.at[1], other)

    def gathered(dst, recvs):
        arrived(has_rest, dst, rest_slot, recvs)
        arrived(has_relay, dst, 1, recvs)

    send_near(state, states, state_send, state_recv)
    send_far(state, states, state_send, state_recv, c == 0)
    for d in (2, y_chips - 2):
        signal_if(block > 0, ring_sem, (z, c, column_head(d)))
    for j in range(1, REACH + 1):
        signal_if((block >= j) & ((c == 1) if j == REACH else True), later_sem, (*place(block - j), h))

    loads[3].wait()
    at_t = lax.broadcasted_iota(jnp.int32, (tokens, tokens), 0)
    at_s = lax.broadcasted_iota(jnp.int32, (tokens, tokens), 1)
    own_seen = (at_t >= at_s) & (doc_col == doc_row)
    for cols in head_cols:
        intra = jnp.where(own_seen, matmul_nt(q[:, cols], k[:, cols]), 0.0).astype(BF16)
        mixed[:, cols] = matmul(intra, v[:, cols])
    loads[4].wait()
    loads[5].wait()
    for i, cols in enumerate(head_cols):
        gates[:, cols] = jax.nn.sigmoid(g[:, cols].astype(F32)) * gain[i : i + 1].astype(F32)

    pl.when(((c == 0) & (z >= 2)) | ((c == 1) & (z + 2 < groups)))(lambda: pl.semaphore_wait(hop_sem, 1))
    send_far(state, states, state_send, state_recv, c == 1)
    signal_if((c == 0) & (z >= 2), later_sem, (z - 2, 1, h))
    gather(states, state_send, state_recv)
    gathered(states, state_recv)
    loads[6].wait()
    spread(sk, keys, key_send, key_recv)
    doc_rows = [states[j, columns : columns + 1, :].astype(F32) for j in range(REACH)]
    for cols in head_cols:
        carried = None
        for j in range(REACH):
            last = doc_rows[j][:, tokens - 1 :]
            part = jnp.where(doc_col == last, matmul(q[:, cols], states[j, cols, :]), 0.0)
            carried = part if carried is None else carried + part
        mixed[:, cols] += carried

    square = mixed[...] * mixed[...]
    own_row[...] = matmul_nt(jnp.ones((8, heads * DH), BF16), square.astype(BF16))[:1]

    pl.when(block > 0)(lambda: pl.semaphore_wait(ring_sem, 2))
    pl.when(first)(lambda: pl.semaphore_wait(barrier, len(near_heads) + len(far_heads)))
    for d in sorted(range(1, y_chips), key=lambda d: abs(d - y_chips // 2)):
        remote(own_row, rows_y.at[y], y_send, y_recv, (z, c, column_head(d))).start()
    rows_y[y] = own_row[...]
    mid[...] = (mixed[...] * gates[...]).astype(BF16)
    spread(mid, mids, mid_send, mid_recv)
    gather(keys, key_send, key_recv, c == 0)

    y_span = rows_y.at[pl.ds(0, y_chips - 1)]
    pltpu.make_async_copy(y_span, y_span, y_recv).wait()
    column_row = rows_x.at[0, x]
    column_row[...] = jnp.sum(rows_y[...], axis=0)
    after = jnp.minimum(REACH, blocks - 1 - block)
    pl.when(after > 0)(lambda: pl.semaphore_wait(later_sem, after))
    for j in range(REACH + 1):

        @pl.when(block + j < blocks)
        def _(j=j):
            for d in (2, 1, 3) + ((0,) if j else ()):
                device = (*place(block + j), row_head(d))
                remote(column_row, rows_x.at[j, x], x_send.at[j], x_recv.at[j], device).start()

    gather(keys, key_send, key_recv, c == 1)
    gather(mids, mid_send, mid_recv)

    loads[7].wait()
    gathered(keys, key_recv)
    scale = 1.0 / math.sqrt(DH)
    for i, cols in enumerate(head_cols):
        query = sq[:, cols]
        parts = [jnp.where(own_seen, matmul_nt(query, sk[:, cols]) * scale, -jnp.inf)]
        for j in range(REACH):
            seen = doc_col == doc_rows[j]
            parts.append(jnp.where(seen, matmul_nt(query, keys[j, :, cols]) * scale, -jnp.inf))
        top = jnp.maximum(jnp.maximum(parts[0], parts[1]), jnp.maximum(parts[2], parts[3]))
        top = jnp.max(top, axis=1, keepdims=True)
        parts = [jnp.exp(part - top) for part in parts]
        total = jnp.sum(parts[0] + parts[1] + parts[2] + parts[3], axis=1, keepdims=True)
        for j, part in enumerate(parts):
            weights[i, j] = part / total

    def x_span(j):
        return rows_x.at[j, pl.ds(0, x_chips if j else x_chips - 1)]

    def inverse_norm(j):
        pl.when(block >= j)(pltpu.make_async_copy(x_span(j), x_span(j), x_recv.at[j]).wait)
        return lax.rsqrt(jnp.sum(rows_x[j], axis=0) / total_columns + 1e-05)

    inverse = inverse_norm(0)
    inverse_col = column(inverse)
    for cols in head_cols:
        out[0, :, cols] = (mixed[:, cols] * gates[:, cols] * inverse_col).astype(BF16)

    def attend(j, values):
        norm = inverse if j == 0 else inverse_norm(j)
        return [matmul((weights[i, j] * norm).astype(BF16), values[:, cols]) for i, cols in enumerate(head_cols)]

    results = attend(0, mid)
    gathered(mids, mid_recv)
    for j in range(REACH, 0, -1):
        results = [result + part for result, part in zip(results, attend(j, mids.at[j - 1]))]
    for result, cols in zip(results, head_cols):
        out[1, :, cols] = result.astype(BF16)

    for condition, copy in waits:
        pl.when(condition)(copy.wait_send)
    pltpu.make_async_copy(y_span, y_span, y_send).wait()
    for j in range(REACH + 1):
        pl.when(block + j < blocks)(pltpu.make_async_copy(x_span(j), x_span(j), x_send.at[j]).wait)


def per_device(mesh, *args):
    q, k, v, g, gain, seg, sq, sk = args
    tokens, columns = q.shape
    groups = mesh.shape["outer"]
    x_chips = min(X_CHIPS, mesh.shape["heads"])
    y_chips = mesh.shape["heads"] // x_chips
    total_columns = columns * mesh.shape["heads"]
    seg = seg.reshape(1, tokens)
    gain = gain.reshape(columns // DH, DH)
    dma = pltpu.SemaphoreType.DMA
    regular = pltpu.SemaphoreType.REGULAR
    block = (tokens, columns)
    stacked = (columns + 16, DH)
    outs = pl.pallas_call(
        functools.partial(kernel, groups, x_chips, y_chips, total_columns),
        out_shape=pltpu.VMEM((2,) + block, BF16),
        in_specs=[pl.BlockSpec(memory_space=pl.ANY)] * 8,
        out_specs=pl.BlockSpec(memory_space=pltpu.VMEM),
        scratch_shapes=[
            pltpu.VMEM(block, BF16), pltpu.VMEM(block, BF16), pltpu.VMEM(block, BF16), pltpu.VMEM(block, BF16),
            pltpu.VMEM((columns // DH, DH), BF16), pltpu.VMEM((1, tokens), jnp.int32),
            pltpu.VMEM(block, BF16), pltpu.VMEM(block, BF16),
            pltpu.VMEM(stacked, BF16), pltpu.VMEM((REACH,) + stacked, BF16),
            pltpu.VMEM((REACH,) + block, BF16),
            pltpu.VMEM(block, BF16), pltpu.VMEM((REACH,) + block, BF16),
            pltpu.VMEM((1, tokens), F32),
            pltpu.VMEM((y_chips, 1, tokens), F32),
            pltpu.VMEM((REACH + 1, x_chips, 1, tokens), F32),
            pltpu.VMEM(block, F32), pltpu.VMEM(block, F32),
            pltpu.VMEM((columns // DH, REACH + 1, tokens, tokens), F32),
            dma((8,)),
            dma((3,)), dma((REACH,)), dma((3,)), dma((REACH,)), dma((3,)), dma((REACH,)),
            dma, dma, dma((REACH + 1,)), dma((REACH + 1,)),
            regular, regular, regular, regular,
        ],
        compiler_params=pltpu.CompilerParams(collective_id=0, has_side_effects=True),
    )(q, k, v, g, gain, seg, sq, sk)
    return outs[0], outs[1]


def solution(mesh):
    block = P(("outer", "inner"), "heads")
    return jax.shard_map(
        functools.partial(per_device, mesh),
        mesh=mesh,
        in_specs=(block, block, block, block, P("heads"), P(("outer", "inner")), block, block),
        out_specs=(block, block),
        check_vma=False,
    )
```
